256 devices in a mesh: dp: 2 (over core), seq: 4 (over y), expert: 32 (over x, z).
Axes of the slice: x: 4, y: 4, z: 8, core: 2. Of those that a mesh axis runs over, the one named last changes fastest.
Arguments:
- query_input: bfloat16 [64, 512, 1024], P(('dp', 'expert'), 'seq'), may hold values from -6 to 6
- key_input: bfloat16 [64, 512, 1024], P(('dp', 'expert'), 'seq'), may hold values from -6 to 6
- value_input: bfloat16 [64, 512, 1024], P(('dp', 'expert'), 'seq'), may hold values from -6 to 6
- routes: int32 [64, 512, 2], P(('dp', 'expert'), 'seq'), may hold values from 0 to 31, all different within a row; in each aligned block of 128 rows (0 to 127, 128 to 255, ..., all dimensions but the last counted through in order) at most 12 rows name the same one
- gate_values: float32 [64, 512, 2], P(('dp', 'expert'), 'seq'), may hold values from 0.2 to 1
- up_weight: bfloat16 [32, 1024, 2048], P('expert'), may hold values from -0.1875 to 0.1875
- down_weight: bfloat16 [32, 2048, 1024], P('expert'), may hold values from -0.125 to 0.125
- cotangent: bfloat16 [64, 512, 1024], P(('dp', 'expert'), 'seq'), may hold values from -6 to 6
Outputs:
- layer_output: bfloat16 [64, 512, 1024], P(('dp', 'expert'), 'seq')
- grad_queries: bfloat16 [64, 512, 1024], P(('dp', 'expert'), 'seq')
- grad_keys: bfloat16 [64, 512, 1024], P(('dp', 'expert'), 'seq')
- grad_values: bfloat16 [64, 512, 1024], P(('dp', 'expert'), 'seq')
- grad_up: float32 [32, 1024, 2048], P('expert', ('dp', 'seq'))
- grad_down: float32 [32, 2048, 1024], P('expert', None, ('dp', 'seq'))
The draws below stay inside these ranges and needn't reach their ends.
Inputs may be any that keep to these rules, and one draw needn't show every extreme that they name: `routes`: each token names 2 different experts. The 128 tokens of one device (aligned blocks of rows) name any one expert at most 12 times, and in every draw some device's tokens name some expert exactly 12 times.
All inputs are finite; a program needn't handle non-finite values.
Results may differ from the reference program's by a relative error of at most 0.017.
Values may be sent and summed in bfloat16 or wider, within the bound.
No kernel may reach another device: no remote copies, remote signals or barrier semaphores. Data moves between devices by JAX's collectives and lax.ppermute only.
A program may use at most 128 MiB of HBM per device.

```python
import math
import jax
import jax.numpy as jnp
import numpy as np
from jax import lax

D = 1024
HEADS = 8
DH = 128
HID = 2048
TOP = 2
TOK_DEV = 128
L = 512
SEQS = 64
EXPERTS = 32
CAP = 12
N_SEQ = 4


def draw_query_input(key, part):
    normal_rows = jax.random.normal(jax.random.fold_in(key, 1), (SEQS, L, D), jnp.float32)
    return jnp.clip(1.5 * normal_rows, -6.0, 6.0).astype(jnp.bfloat16)


def draw_key_input(key, part):
    normal_rows = jax.random.normal(jax.random.fold_in(key, 5), (SEQS, L, D), jnp.float32)
    return jnp.clip(1.5 * normal_rows, -6.0, 6.0).astype(jnp.bfloat16)


def block_levels(own_key, extent, split, low, top_value):
    gain = 1.0
    for dim, shards_of in split:
        draws = jax.random.uniform(jax.random.fold_in(jax.random.fold_in(own_key, 6), dim), (shards_of,), jnp.float32, low / len(split), top_value / len(split))
        gain = gain * jnp.repeat(jnp.exp(draws), extent[dim] // shards_of).reshape((-1,) + (1,) * (len(extent) - 1 - dim))
    return gain


def assign_block(key, own, number, rows, number_of, top, bound, slope):
    order = jax.random.permutation(key, number_of)
    crowded, ordinary = shares(number_of, rows * top, bound, slope, True), shares(number_of, rows * top, bound, slope, False)
    places = jnp.arange(number_of)

    def named(sizes, rotation):
        used = int((sizes > 0).sum())
        fixed = max(1, used // 4)
        passed = fixed + (places - fixed + rotation * (used - fixed)) % max(1, number_of - fixed)
        return jnp.zeros((number_of,), jnp.int32).at[order[jnp.where(places < fixed, places, passed)]].set(jnp.asarray(sizes, jnp.int32))

    sizes = jnp.where(number % 4 == 0, named(crowded, number // 4), named(ordinary, number - number // 4 - 1))
    mixed = jax.random.permutation(jax.random.fold_in(own, 3), number_of)
    donor, sink = mixed[0:number_of // 2 * 2:2], mixed[1:number_of // 2 * 2:2]
    room = jnp.minimum(sizes[donor] - 1, bound - sizes[sink]) // 2
    room = jnp.where((donor == order[0]) | (sink == order[0]) | (sizes[sink] == 0), 0, jnp.maximum(room, 0))
    passed = jax.random.randint(jax.random.fold_in(own, 4), (number_of // 2,), 0, 1 << 20) % (room + 1)
    sizes = sizes.at[donor].add(-passed).at[sink].add(passed)
    members = jnp.searchsorted(jnp.cumsum(sizes), jnp.arange(rows * top), side="right").astype(jnp.int32)
    listing = members.reshape(top, rows).T
    listing = listing[jax.random.permutation(jax.random.fold_in(own, 1), rows)]
    rotation = jax.random.randint(jax.random.fold_in(own, 2), (rows, 1), 0, top)
    return jnp.take_along_axis(listing, (jnp.arange(top)[None, :] + rotation) % top, axis=1)


def shares(number_of, total, bound, lean, full):
    portions = [(1 << 20) // math.isqrt(grade ** lean) + 1 for grade in range(1, number_of + 1)]
    largest = bound if full else min(bound, max(-(-total // number_of), total * portions[0] // sum(portions)))
    least = 1 if total - largest >= number_of - 1 else 0
    holding, rest = [largest] + [least] * (number_of - 1), total - largest - least * (number_of - 1)
    while rest > 0:
        movable = [i for i in range(1, number_of) if holding[i] < largest] or [i for i in range(1, number_of) if holding[i] < bound]
        mass, remaining = sum([portions[i] for i in movable]), rest
        for i in movable:
            extra = min(bound - holding[i], max(1, remaining * portions[i] // mass), rest)
            holding[i] = holding[i] + extra
            rest = rest - extra
    return np.array(holding)


def scatter_about(own_key, dims, width, limit, shards=(), held_as=jnp.bfloat16):
    array = jax.random.normal(own_key, dims, jnp.float32) * width
    if len(shards) > 0:
        array = block_levels(own_key, dims, shards, -0.22, 0.18) * array
    return jnp.clip(array, min=-limit, max=limit).astype(held_as)


def setup_inputs(seed: int = 0) -> dict:
    keys = jax.random.split(jax.random.key(seed), 9)
    query_input = draw_query_input(jax.random.fold_in(keys[8], 71), 0)
    key_input = draw_key_input(jax.random.fold_in(keys[8], 71), 0)
    value_input = scatter_about(keys[2], (SEQS, L, D), 1.0, 6.0, ((0, 64), (1, 4)))
    routes_keys = jax.random.split(jax.random.fold_in(keys[3], 1), SEQS * L // TOK_DEV)
    routes_turns = jax.random.permutation(jax.random.fold_in(keys[3], 3), SEQS * L // TOK_DEV)
    routes = jax.vmap(lambda own, number: assign_block(jax.random.fold_in(keys[3], 2), own, number, TOK_DEV, EXPERTS, TOP, CAP, 2))(routes_keys, routes_turns).reshape((SEQS, L, TOP))
    gate_values = jnp.clip(0.2 + 0.8 * jax.random.uniform(keys[4], (SEQS, L, TOP), jnp.float32) ** block_levels(keys[4], (SEQS, L, TOP), ((0, 64), (1, 4)), -0.2, 0.2), 0.2, 1.0)
    up_weight = scatter_about(keys[5], (EXPERTS, D, HID), D ** -0.5, 0.1875, ((0, 32),))
    down_weight = scatter_about(keys[6], (EXPERTS, HID, D), HID ** -0.5, 0.125, ((0, 32),))
    cotangent = scatter_about(keys[7], (SEQS, L, D), 1.0, 6.0, ((0, 64), (1, 4)))
    return {"query_input": query_input, "key_input": key_input, "value_input": value_input, "routes": routes, "gate_values": gate_values, "up_weight": up_weight, "down_weight": down_weight, "cotangent": cotangent}


EPSILON = 1e-06
GELU_COEF = math.sqrt(2.0 / math.pi)

def gelu_pair(inputs):
    cubic = inputs + 0.044715 * inputs * inputs * inputs
    hyper = jnp.tanh(GELU_COEF * cubic)
    result = 0.5 * inputs * (1.0 + hyper)
    slope_value = 0.5 * (1.0 + hyper) + 0.5 * inputs * (1.0 - hyper * hyper) * GELU_COEF * (1.0 + 3.0 * 0.044715 * inputs * inputs)
    return (result, slope_value)

def prob_table(query_rows, key_rows):
    scaling = 1.0 / math.sqrt(DH)
    scores = jnp.einsum('qhd,khd->hqk', query_rows.astype(jnp.float32), key_rows.astype(jnp.float32)) * scaling
    highest = lax.optimization_barrier(jnp.max(scores, axis=-1, keepdims=True))
    exponent = jnp.exp(scores - highest)
    return exponent / lax.optimization_barrier(jnp.sum(exponent, axis=-1, keepdims=True))

def split_heads(tensor):
    return tensor.reshape(L, HEADS, DH)

def attend_forward(triple):
    query_rows = split_heads(triple[0])
    key_rows = split_heads(triple[1])
    value_rows = split_heads(triple[2])
    prob_rows = prob_table(query_rows, key_rows)
    prob_bf = prob_rows.astype(jnp.bfloat16)
    output = jnp.einsum('hqk,khd->qhd', prob_bf.astype(jnp.float32), value_rows.astype(jnp.float32))
    return output.astype(jnp.bfloat16).reshape(L, D)

def attend_backward(quad):
    query_rows = split_heads(quad[0])
    key_rows = split_heads(quad[1])
    value_rows = split_heads(quad[2])
    upstream = split_heads(quad[3])
    scaling = 1.0 / math.sqrt(DH)
    prob_rows = prob_table(query_rows, key_rows)
    prob_bf = prob_rows.astype(jnp.bfloat16)
    grad_probs = jnp.einsum('qhd,khd->hqk', upstream.astype(jnp.float32), value_rows.astype(jnp.float32))
    row_delta = lax.optimization_barrier(jnp.sum(prob_rows * grad_probs, axis=-1, keepdims=True))
    grad_scores = (prob_rows * (grad_probs - row_delta) * scaling).astype(jnp.bfloat16)
    grad_query = jnp.einsum('hqk,khd->qhd', grad_scores.astype(jnp.float32), key_rows.astype(jnp.float32))
    grad_key = jnp.einsum('hqk,qhd->khd', grad_scores.astype(jnp.float32), query_rows.astype(jnp.float32))
    grad_value = jnp.einsum('hqk,qhd->khd', prob_bf.astype(jnp.float32), upstream.astype(jnp.float32))
    return (grad_query.astype(jnp.bfloat16).reshape(L, D), grad_key.astype(jnp.bfloat16).reshape(L, D), grad_value.astype(jnp.bfloat16).reshape(L, D))

def reference(query_input, key_input, value_input, routes, gate_values, up_weight, down_weight, cotangent):
    attended = lax.map(attend_forward, (query_input, key_input, value_input))
    token_count = SEQS * L
    attended_f = attended.reshape(token_count, D).astype(jnp.float32)
    inverse_rms = lax.rsqrt(lax.optimization_barrier(jnp.mean(attended_f * attended_f, axis=-1, keepdims=True)) + EPSILON)
    unit_rows = attended_f * inverse_rms
    normed = unit_rows.astype(jnp.bfloat16)
    chosen = routes.reshape(-1).astype(jnp.int32)
    gate_rows = gate_values.reshape(token_count, TOP).astype(jnp.float32)
    upstream = cotangent.reshape(token_count, D).astype(jnp.float32)
    grad_out_rows = (gate_rows[:, :, None] * upstream[:, None, :]).astype(jnp.bfloat16).reshape(token_count * TOP, D)
    room_rows = SEQS * N_SEQ * CAP

    def per_expert(running, expert):
        out_acc, grad_acc = running
        picked = jnp.argsort((chosen != expert).astype(jnp.int32), stable=True)[:room_rows].astype(jnp.int32)
        live_mask = (chosen[picked] == expert)[:, None]
        rows_in = jnp.where(live_mask, normed[picked // TOP], jnp.zeros((), jnp.bfloat16))
        grads_in = jnp.where(live_mask, grad_out_rows[picked], jnp.zeros((), jnp.bfloat16))
        weight_in = up_weight[expert]
        weight_out = down_weight[expert]
        pre_act = jnp.dot(rows_in, weight_in, preferred_element_type=jnp.float32)
        act_value, act_slope = gelu_pair(pre_act)
        activated = act_value.astype(jnp.bfloat16)
        produced = jnp.dot(activated, weight_out, preferred_element_type=jnp.float32).astype(jnp.bfloat16)
        grad_act = jnp.dot(grads_in, weight_out.T, preferred_element_type=jnp.float32)
        grad_pre = (grad_act * act_slope).astype(jnp.bfloat16)
        grad_down_e = jnp.dot(activated.T, grads_in, preferred_element_type=jnp.float32)
        grad_up_e = jnp.dot(rows_in.T, grad_pre, preferred_element_type=jnp.float32)
        grad_normed = jnp.dot(grad_pre, weight_in.T, preferred_element_type=jnp.float32).astype(jnp.bfloat16)
        out_acc = out_acc.at[picked].add(jnp.where(live_mask, produced, jnp.zeros((), jnp.bfloat16)))
        grad_acc = grad_acc.at[picked].add(jnp.where(live_mask, grad_normed, jnp.zeros((), jnp.bfloat16)))
        return ((out_acc, grad_acc), (grad_up_e, grad_down_e))
    start_rows = jnp.zeros((token_count * TOP, D), jnp.bfloat16)
    (out_acc, grad_acc), (grad_up, grad_down) = lax.scan(per_expert, (start_rows, start_rows), jnp.arange(EXPERTS, dtype=jnp.int32))
    returned = out_acc.reshape(token_count, TOP, D).astype(jnp.float32)
    expert_mix = lax.optimization_barrier(jnp.sum(gate_rows[:, :, None] * returned, axis=1))
    layer_output = (attended_f + expert_mix).astype(jnp.bfloat16).reshape(SEQS, L, D)
    grad_unit = lax.optimization_barrier(jnp.sum(grad_acc.reshape(token_count, TOP, D).astype(jnp.float32), axis=1))
    grad_attended = upstream + inverse_rms * (grad_unit - unit_rows * lax.optimization_barrier(jnp.mean(grad_unit * unit_rows, axis=-1, keepdims=True)))
    grad_attended = grad_attended.astype(jnp.bfloat16).reshape(SEQS, L, D)
    grad_queries, grad_keys, grad_values = lax.map(attend_backward, (query_input, key_input, value_input, grad_attended))
    return (layer_output, grad_queries, grad_keys, grad_values, grad_up, grad_down)
```

```python
import functools
import math

import jax
import jax.numpy as jnp
from jax import lax
from jax.experimental import pallas as pl
from jax.experimental.pallas import tpu as pltpu
from jax.sharding import PartitionSpec as P

DH = 128
TOP = 2
EPSILON = 1e-06
GELU_COEF = math.sqrt(2.0 / math.pi)
BF = jnp.bfloat16
F32 = jnp.float32
VMEM = pl.BlockSpec(memory_space=pltpu.VMEM)
SMEM = pl.BlockSpec(memory_space=pltpu.SMEM)
NN = (((1,), (0,)), ((), ()))
NT = (((1,), (1,)), ((), ()))
TN = (((0,), (0,)), ((), ()))
HEAVY = pl.CostEstimate(flops=1_000_000_000_000, transcendentals=0, bytes_accessed=1_000_000)
BIG = pltpu.CompilerParams(vmem_limit_bytes=56 * 1024 * 1024)


def dot(a, b, dims=NN):
    return lax.dot_general(a, b, dims, preferred_element_type=F32)


def sds(shape, dtype):
    return jax.ShapeDtypeStruct(shape, dtype)


def lane_block(me, step, parts, width):
    return pl.ds(pl.multiple_of(lax.rem(me + step, parts) * width, width), width)


def split_kernel(parts, me_ref, q_ref, k_ref, v_ref, *outs):
    me = me_ref[0]
    rows = q_ref.shape[0]
    width = q_ref.shape[1] // parts
    for step in range(parts):
        lanes = lane_block(me, step, parts, width)
        for i, ref in enumerate((q_ref, k_ref, v_ref)):
            outs[step][i * rows:(i + 1) * rows, :] = ref[:, lanes]


def join_kernel(parts, me_ref, *refs):
    me = me_ref[0]
    pieces, outs = refs[:parts], refs[parts:]
    rows = outs[0].shape[0]
    width = outs[0].shape[1] // parts
    for step in range(parts):
        lanes = lane_block(me, step, parts, width)
        for i, ref in enumerate(outs):
            ref[:, lanes] = pieces[step][i * rows:(i + 1) * rows, :]


def attend_kernel(parts, *refs):
    pieces = refs[:parts]
    outs = refs[parts:2 * parts]
    probs_ref, keys, values = refs[2 * parts:]
    rows = outs[0].shape[0]
    width = outs[0].shape[1]
    scaling = 1.0 / math.sqrt(DH)
    for step in range(parts):
        keys[step * rows:(step + 1) * rows, :] = pieces[step][rows:2 * rows, :]
        values[step * rows:(step + 1) * rows, :] = pieces[step][2 * rows:3 * rows, :]
    for head in range(width // DH):
        lanes = slice(head * DH, (head + 1) * DH)
        for step in range(parts):
            scores = dot(pieces[step][0:rows, lanes], keys[:, lanes], NT) * scaling
            exponent = jnp.exp(scores - jnp.max(scores, axis=-1, keepdims=True))
            probs = exponent / jnp.sum(exponent, axis=-1, keepdims=True)
            probs_ref[head, step * rows:(step + 1) * rows, :] = probs
            outs[step][:, lanes] = dot(probs.astype(BF), values[:, lanes]).astype(BF)


def attend_back_kernel(parts, *refs):
    pieces = refs[:parts]
    grads = refs[parts:2 * parts]
    probs_ref = refs[2 * parts]
    outs = refs[2 * parts + 1:3 * parts + 1]
    keys, values, grad_keys, grad_values = refs[3 * parts + 1:]
    rows = grads[0].shape[0]
    width = grads[0].shape[1]
    scaling = 1.0 / math.sqrt(DH)
    for step in range(parts):
        keys[step * rows:(step + 1) * rows, :] = pieces[step][rows:2 * rows, :]
        values[step * rows:(step + 1) * rows, :] = pieces[step][2 * rows:3 * rows, :]
    for head in range(width // DH):
        lanes = slice(head * DH, (head + 1) * DH)
        for step in range(parts):
            query = pieces[step][0:rows, lanes]
            grad = grads[step][:, lanes]
            probs = probs_ref[head, step * rows:(step + 1) * rows, :]
            grad_probs = dot(grad, values[:, lanes], NT)
            delta = jnp.sum(probs * grad_probs, axis=-1, keepdims=True)
            grad_scores = (probs * (grad_probs - delta) * scaling).astype(BF)
            outs[step][0:rows, lanes] = dot(grad_scores, keys[:, lanes]).astype(BF)
            key_part = dot(grad_scores, query, TN)
            value_part = dot(probs.astype(BF), grad, TN)
            if step == 0:
                grad_keys[:, lanes] = key_part
                grad_values[:, lanes] = value_part
            else:
                grad_keys[:, lanes] += key_part
                grad_values[:, lanes] += value_part
    for step in range(parts):
        outs[step][rows:2 * rows, :] = grad_keys[step * rows:(step + 1) * rows, :].astype(BF)
        outs[step][2 * rows:3 * rows, :] = grad_values[step * rows:(step + 1) * rows, :].astype(BF)


def chunk_of(array, c):
    return array[:, c * 128:(c + 1) * 128]


def lane_cat(pieces):
    return jnp.concatenate(pieces, axis=1)


def half_pickers(owners):
    shape = (owners * 4, owners * 8)
    row = lax.broadcasted_iota(jnp.int32, shape, 0)
    col = lax.broadcasted_iota(jnp.int32, shape, 1)
    first = lax.shift_left(lax.shift_right_logical(row, 2), 3) + lax.bitwise_and(row, 3)
    return [(col == first + 4 * half).astype(F32).astype(BF) for half in range(2)]


def read_tiles(ref):
    owners, lines, _ = ref.shape
    tiles = [
        ref[:, 8 * t:8 * t + 8, :].astype(F32).reshape(owners * 8, 128).astype(BF)
        for t in range(lines // 8)
    ]
    count = len(tiles) * 2 // 3
    return tiles[:count], lane_cat(tiles[count:])


def write_tiles(ref, low, high):
    owners = ref.shape[0]
    count = low.shape[1] // 128
    for c in range(count):
        ref[:, 8 * c:8 * c + 8, :] = chunk_of(low, c).reshape(owners, 8, 128).astype(BF)
    for c in range(count // 2):
        start = 8 * (count + c)
        ref[:, start:start + 8, :] = chunk_of(high, c).reshape(owners, 8, 128).astype(BF)


def split_parity(array):
    count = array.shape[1] // 128
    return [lane_cat([chunk_of(array, c) for c in range(half, count, 2)]) for half in range(2)]


def merge_parity(even, odd):
    count = even.shape[1] // 128
    return lane_cat([chunk_of(part, c) for c in range(count) for part in (even, odd)])


def unpack_rows(ref, out_ref):
    low, high = read_tiles(ref)
    owners = ref.shape[0]
    even, odd = [dot(pick, high).astype(BF) for pick in half_pickers(owners)]
    out_ref[0:owners * 8, :] = lane_cat(low)
    out_ref[owners * 8:, :] = merge_parity(even, odd)


def pack_rows(rows, ref):
    owners = ref.shape[0]
    pickers = half_pickers(owners)
    parts = split_parity(rows[owners * 8:, :].astype(BF))
    high = dot(pickers[0], parts[0], TN) + dot(pickers[1], parts[1], TN)
    write_tiles(ref, rows[0:owners * 8, :], high)


def pack_tokens(places, arrays, ref):
    low = sum([dot(place[0], x) for place, x in zip(places, arrays)])
    high = None
    for place, x in zip(places, arrays):
        for half, part in enumerate(split_parity(x)):
            term = dot(place[1 + half], part)
            high = term if high is None else high + term
    write_tiles(ref, low, high)


def unpack_tokens(place, low, high):
    even, odd = [dot(place[1 + half], high, TN) for half in range(2)]
    return dot(place[0], lane_cat(low), TN) + merge_parity(even, odd)


def column(row):
    side = row.shape[1]
    return jnp.broadcast_to(row, (side, side)).T[:, 0:1]


def place_kernel(experts, routes_ref, gates_ref, cot_ref, place_ref, packed_ref):
    tokens = cot_ref.shape[0]
    first = lax.broadcasted_iota(jnp.int32, (tokens, tokens), 0)
    second = lax.broadcasted_iota(jnp.int32, (tokens, tokens), 1)
    earlier = (first < second).astype(F32).astype(BF)
    expert_ids = lax.broadcasted_iota(jnp.int32, (experts, tokens), 0)
    line_ids = lax.broadcasted_iota(jnp.int32, (experts * 8, tokens), 0)
    routes = [routes_ref[j:j + 1, :] for j in range(TOP)]
    hits = [(route == expert_ids).astype(F32) for route in routes]
    before = dot(sum(hits[1:], hits[0]).astype(BF), earlier)
    upstream = cot_ref[...].astype(F32)
    places, arrays = [], []
    for j in range(TOP):
        rank = jnp.sum(before * hits[j], axis=0, keepdims=True).astype(jnp.int32)
        line = routes[j] * 8 + rank
        targets = (
            jnp.where(rank < 8, line, -1),
            jnp.where(rank >= 8, line - 8, -1),
            jnp.where(rank >= 8, line - 4, -1),
        )
        place = [(line_ids == target).astype(F32).astype(BF) for target in targets]
        for i, part in enumerate(place):
            place_ref[j, i] = part
        places.append(place)
        arrays.append((column(gates_ref[j:j + 1, :]) * upstream).astype(BF))
    pack_tokens(places, arrays, packed_ref)


def inverse_rms_of(attended):
    return lax.rsqrt(jnp.mean(attended * attended, axis=-1, keepdims=True) + EPSILON)


def joint_place(place_ref):
    joint = []
    for i in range(3):
        part = place_ref[0, i]
        for j in range(1, TOP):
            part = part + place_ref[j, i]
        joint.append(part)
    return joint


def norm_kernel(parts, me_ref, place_ref, *refs):
    pieces, (attended_ref, packed_ref) = refs[:parts], refs[parts:]
    me = me_ref[0]
    width = pieces[0].shape[1]
    for step in range(parts):
        attended_ref[:, lane_block(me, step, parts, width)] = pieces[step][...]
    attended = attended_ref[...].astype(F32)
    normed = (attended * inverse_rms_of(attended)).astype(BF)
    pack_tokens([joint_place(place_ref)], [normed], packed_ref)


def turn_rows(pairs, parts, rows_ref, turned_ref):
    band = rows_ref.shape[1] // (pairs * parts)
    for s in range(pairs * parts):
        block = (s % pairs) * parts + s // pairs
        turned_ref[s * band:(s + 1) * band, :] = rows_ref[:, block * band:(block + 1) * band].T


def dact_kernel(pairs, parts, packed_ref, down_ref, out_ref, turned_ref, rows):
    @pl.when(pl.program_id(0) == 0)
    def _():
        unpack_rows(packed_ref, rows)
        turn_rows(pairs, parts, rows, turned_ref)

    out_ref[...] = dot(rows[...], down_ref[...], NT)


def expert_kernel(packed_ref, up_ref, dact_ref, hidden_ref, rows_ref, dnormed_ref, total):
    step = pl.program_id(0)

    @pl.when(step == 0)
    def _():
        unpack_rows(packed_ref, rows_ref)

    chunk = up_ref.shape[1]
    part = None
    for start in range(0, chunk, 256):
        lanes = slice(start, start + 256)
        weights = up_ref[:, lanes]
        pre = dot(rows_ref[...], weights)
        square = pre * pre
        hyper = jnp.tanh(GELU_COEF * (pre + 0.044715 * pre * square))
        hidden_ref[0, :, lanes] = (0.5 * pre * (1.0 + hyper)).astype(BF)
        slope = 0.5 * (1.0 + hyper) + 0.5 * pre * (1.0 - hyper * hyper) * GELU_COEF * (
            1.0 + 3.0 * 0.044715 * square
        )
        dpre = (dact_ref[:, lanes] * slope).astype(BF)
        hidden_ref[1, :, lanes] = dpre
        term = dot(dpre, weights, NT)
        part = term if part is None else part + term

    @pl.when(step == 0)
    def _():
        total[...] = part

    @pl.when(step > 0)
    def _():
        total[...] += part

    @pl.when(step == pl.num_programs(0) - 1)
    def _():
        pack_rows(total[...], dnormed_ref)


def tail_kernel(pairs, parts, blocks, hidden_ref, down_ref, turned_ref, rows_ref, grads_ref, packed_ref, turned, total):
    step = pl.program_id(0)

    @pl.when(step < blocks)
    def _():
        act = hidden_ref[0]
        grads_ref[...] = dot(turned_ref[...], act).astype(BF)
        part = dot(act, down_ref[...])

        @pl.when(step == 0)
        def _():
            total[...] = part

        @pl.when(step > 0)
        def _():
            total[...] += part

    @pl.when(step == blocks)
    def _():
        pack_rows(total[...], packed_ref)
        turn_rows(pairs, parts, rows_ref, turned)

    @pl.when(step >= blocks)
    def _():
        grads_ref[...] = dot(turned[...], hidden_ref[0]).astype(BF)


def dattended_kernel(parts, me_ref, place_ref, back_ref, attended_ref, cot_ref, *refs):
    outs, full = refs[:parts], refs[parts]
    me = me_ref[0]
    low, high = read_tiles(back_ref)
    grad_unit = unpack_tokens(joint_place(place_ref), low, high)
    attended = attended_ref[...].astype(F32)
    inverse_rms = inverse_rms_of(attended)
    unit = attended * inverse_rms
    grad = cot_ref[...].astype(F32) + inverse_rms * (
        grad_unit - unit * jnp.mean(grad_unit * unit, axis=-1, keepdims=True)
    )
    full[...] = grad.astype(BF)
    width = outs[0].shape[1]
    for step in range(parts):
        outs[step][...] = full[:, lane_block(me, step, parts, width)]


def mix_kernel(place_ref, back_ref, attended_ref, gates_ref, out_ref):
    low, high = read_tiles(back_ref)
    mix = None
    for j in range(TOP):
        place = [place_ref[j, i] for i in range(3)]
        term = column(gates_ref[j:j + 1, :]) * unpack_tokens(place, low, high)
        mix = term if mix is None else mix + term
    out_ref[...] = (attended_ref[...].astype(F32) + mix).astype(BF)


def widen_kernel(sums_ref, up_out, down_out):
    hidden = up_out.shape[1]
    down_out[...] = sums_ref[:, 0:hidden].astype(F32).T
    up_out[...] = sums_ref[:, hidden:].astype(F32)


def shards(query, key, value, routes, gates, up, down, cotangent):
    tokens, model = query.shape[1:]
    owners = lax.axis_size("expert")
    parts = lax.axis_size("seq")
    pairs = lax.axis_size("dp")
    capacity = tokens * TOP * 3 // (2 * owners)
    slots = owners * capacity
    hidden = up.shape[2]
    width = model // parts
    length = tokens * parts
    heads = width // DH
    up, down = up[0], down[0]
    cot = cotangent[0]
    route, gate = routes[0].T, gates[0].T
    me = jnp.reshape(lax.axis_index("seq"), (1,)).astype(jnp.int32)

    def shift(piece, step):
        pairs_of = [(i, (i + step) % parts) for i in range(parts)]
        return lax.ppermute(piece, "seq", pairs_of)

    def swap(packed):
        return lax.all_to_all(packed, "expert", split_axis=0, concat_axis=0, tiled=True)

    order = (2, 1, 3) if parts == 4 else tuple(range(1, parts))

    def exchange(pieces, sign):
        moved = {step: shift(pieces[step], sign * step) for step in order}
        return [pieces[0]] + [moved[step] for step in range(1, parts)]

    triple = sds((3 * tokens, width), BF)
    single = sds((tokens, width), BF)
    wire = sds((owners, capacity * model // 128, 128), BF)
    sent = pl.pallas_call(
        functools.partial(split_kernel, parts),
        out_shape=[triple] * parts,
        in_specs=[SMEM] + [VMEM] * 3,
        out_specs=[VMEM] * parts,
        name="split_qkv",
    )(me, query[0], key[0], value[0])
    pieces = exchange(sent, 1)

    cot_late, _ = lax.optimization_barrier((cot, sent[0]))
    place, packed_grads = pl.pallas_call(
        functools.partial(place_kernel, owners),
        out_shape=[sds((TOP, 3, owners * 8, tokens), BF), wire],
        in_specs=[VMEM] * 3,
        out_specs=[VMEM] * 2,
        name="place",
    )(route, gate, cot_late)
    grad_wire = swap(packed_grads)

    attended_pieces = pl.pallas_call(
        functools.partial(attend_kernel, parts),
        out_shape=[single] * parts + [sds((heads, length, length), F32)],
        in_specs=[VMEM] * parts,
        out_specs=[VMEM] * (parts + 1),
        scratch_shapes=[pltpu.VMEM((length, width), BF)] * 2,
        compiler_params=BIG,
        name="attend",
    )(*pieces)
    probs = attended_pieces[parts]
    attended_pieces = exchange(attended_pieces[:parts], -1)

    attended, packed = pl.pallas_call(
        functools.partial(norm_kernel, parts),
        out_shape=[sds((tokens, model), BF), wire],
        in_specs=[SMEM] + [VMEM] * (parts + 1),
        out_specs=[VMEM] * 2,
        name="norm_pack",
    )(me, place, *attended_pieces)
    wire_rows = swap(packed)

    blocks = 4
    chunk = hidden // blocks
    whole_wire = pl.BlockSpec(wire.shape, lambda i: (0, 0, 0))
    dact, turned = pl.pallas_call(
        functools.partial(dact_kernel, pairs, parts),
        grid=(blocks,),
        out_shape=[sds((slots, hidden), F32), sds((model, slots), BF)],
        in_specs=[whole_wire, pl.BlockSpec((chunk, model), lambda i: (i, 0))],
        out_specs=[
            pl.BlockSpec((slots, chunk), lambda i: (0, i)),
            pl.BlockSpec((model, slots), lambda i: (0, 0)),
        ],
        scratch_shapes=[pltpu.VMEM((slots, model), BF)],
        compiler_params=BIG,
        name="dact",
    )(grad_wire, down)
    both, rows, dnormed = pl.pallas_call(
        expert_kernel,
        grid=(blocks,),
        out_shape=[sds((2, slots, hidden), BF), sds((slots, model), BF), wire],
        in_specs=[
            whole_wire,
            pl.BlockSpec((model, chunk), lambda i: (0, i)),
            pl.BlockSpec((slots, chunk), lambda i: (0, i)),
        ],
        out_specs=[
            pl.BlockSpec((2, slots, chunk), lambda i: (0, 0, i)),
            pl.BlockSpec((slots, model), lambda i: (0, 0)),
            whole_wire,
        ],
        scratch_shapes=[pltpu.VMEM((slots, model), F32)],
        compiler_params=BIG,
        name="expert",
    )(wire_rows, up, dact)
    dnormed_back = swap(dnormed)

    partial_grads, produced = pl.pallas_call(
        functools.partial(tail_kernel, pairs, parts, blocks),
        grid=(2 * blocks,),
        out_shape=[sds((model, 2 * hidden), BF), wire],
        in_specs=[
            pl.BlockSpec((1, slots, chunk), lambda i: (lax.div(i, blocks), 0, lax.rem(i, blocks))),
            pl.BlockSpec((chunk, model), lambda i: (jnp.minimum(i, blocks - 1), 0)),
            pl.BlockSpec((model, slots), lambda i: (0, 0)),
            pl.BlockSpec((slots, model), lambda i: (0, 0)),
        ],
        out_specs=[pl.BlockSpec((model, chunk), lambda i: (0, i)), whole_wire],
        scratch_shapes=[pltpu.VMEM((model, slots), BF), pltpu.VMEM((slots, model), F32)],
        compiler_params=BIG,
        name="weight_grads",
    )(both, down, turned, rows)
    sums = lax.psum_scatter(partial_grads, ("seq", "dp"), scatter_dimension=0, tiled=True)

    grad_pieces = pl.pallas_call(
        functools.partial(dattended_kernel, parts),
        out_shape=[single] * parts,
        in_specs=[SMEM] + [VMEM] * 4,
        out_specs=[VMEM] * parts,
        scratch_shapes=[pltpu.VMEM((tokens, model), BF)],
        cost_estimate=HEAVY,
        name="dattended",
    )(me, place, dnormed_back, attended, cot)
    grad_pieces = exchange(grad_pieces, 1)

    produced, _ = lax.optimization_barrier((produced, dnormed_back))
    produced_back = swap(produced)

    back_pieces = pl.pallas_call(
        functools.partial(attend_back_kernel, parts),
        out_shape=[triple] * parts,
        in_specs=[VMEM] * (2 * parts + 1),
        out_specs=[VMEM] * parts,
        scratch_shapes=[pltpu.VMEM((length, width), BF)] * 2
        + [pltpu.VMEM((length, width), F32)] * 2,
        compiler_params=BIG,
        name="attend_back",
    )(*pieces, *grad_pieces, probs)
    back_pieces = exchange(back_pieces, -1)

    layer_output = pl.pallas_call(
        mix_kernel,
        out_shape=sds((tokens, model), BF),
        in_specs=[VMEM] * 4,
        out_specs=VMEM,
        name="mix",
    )(place, produced_back, attended, gate)
    grad_queries, grad_keys, grad_values = pl.pallas_call(
        functools.partial(join_kernel, parts),
        out_shape=[sds((tokens, model), BF)] * 3,
        in_specs=[SMEM] + [VMEM] * parts,
        out_specs=[VMEM] * 3,
        name="join_grads",
    )(me, *back_pieces)
    band = model // (pairs * parts)
    grad_up, grad_down = pl.pallas_call(
        widen_kernel,
        out_shape=[sds((band, hidden), F32), sds((hidden, band), F32)],
        in_specs=[VMEM],
        out_specs=[VMEM] * 2,
        name="widen",
    )(sums)
    return (
        layer_output[None],
        grad_queries[None],
        grad_keys[None],
        grad_values[None],
        grad_up[None],
        grad_down[None],
    )


def solution(mesh):
    rows = P(("dp", "expert"), "seq", None)
    weight = P("expert", None, None)
    return jax.shard_map(
        shards,
        mesh=mesh,
        in_specs=(rows, rows, rows, rows, rows, weight, weight, rows),
        out_specs=(rows, rows, rows, rows, P("expert", ("dp", "seq"), None), P("expert", None, ("dp", "seq"))),
        check_vma=False,
    )
```

```python
import functools
import math

import jax
import jax.numpy as jnp
from jax import lax
from jax.experimental import pallas as pl
from jax.experimental.pallas import tpu as pltpu
from jax.sharding import PartitionSpec as P

DH = 128
TOP = 2
EPSILON = 1e-06
GELU_COEF = math.sqrt(2.0 / math.pi)
BF = jnp.bfloat16
F32 = jnp.float32
VMEM = pl.BlockSpec(memory_space=pltpu.VMEM)
SMEM = pl.BlockSpec(memory_space=pltpu.SMEM)
NN = (((1,), (0,)), ((), ()))
NT = (((1,), (1,)), ((), ()))
TN = (((0,), (0,)), ((), ()))
HEAVY = pl.CostEstimate(flops=1_000_000_000_000, transcendentals=0, bytes_accessed=1_000_000)
MIDDLE = pl.CostEstimate(flops=40_000_000_000, transcendentals=0, bytes_accessed=1_000_000)
BIG = pltpu.CompilerParams(vmem_limit_bytes=56 * 1024 * 1024)


def dot(a, b, dims=NN):
    return lax.dot_general(a, b, dims, preferred_element_type=F32)


def sds(shape, dtype):
    return jax.ShapeDtypeStruct(shape, dtype)


def near(array):
    return pltpu.with_memory_space_constraint(array, pltpu.VMEM)


def lane_block(me, step, parts, width):
    return pl.ds(pl.multiple_of(lax.rem(me + step, parts) * width, width), width)


def split_kernel(parts, me_ref, q_ref, k_ref, v_ref, *outs):
    me = me_ref[0]
    rows = q_ref.shape[0]
    width = q_ref.shape[1] // parts
    for step in range(parts):
        lanes = lane_block(me, step, parts, width)
        for i, ref in enumerate((q_ref, k_ref, v_ref)):
            outs[step][i * rows:(i + 1) * rows, :] = ref[:, lanes]


def join_kernel(parts, me_ref, *refs):
    me = me_ref[0]
    pieces, outs = refs[:parts], refs[parts:]
    rows = outs[0].shape[0]
    width = outs[0].shape[1] // parts
    for step in range(parts):
        lanes = lane_block(me, step, parts, width)
        for i, ref in enumerate(outs):
            ref[:, lanes] = pieces[step][i * rows:(i + 1) * rows, :]


def attend_kernel(parts, *refs):
    pieces = refs[:parts]
    outs = refs[parts:2 * parts]
    probs_ref, keys, values = refs[2 * parts:]
    rows = outs[0].shape[0]
    width = outs[0].shape[1]
    scaling = 1.0 / math.sqrt(DH)
    for step in range(parts):
        keys[step * rows:(step + 1) * rows, :] = pieces[step][rows:2 * rows, :]
        values[step * rows:(step + 1) * rows, :] = pieces[step][2 * rows:3 * rows, :]
    for head in range(width // DH):
        lanes = slice(head * DH, (head + 1) * DH)
        for step in range(parts):
            scores = dot(pieces[step][0:rows, lanes], keys[:, lanes], NT) * scaling
            exponent = jnp.exp(scores - jnp.max(scores, axis=-1, keepdims=True))
            probs = exponent / jnp.sum(exponent, axis=-1, keepdims=True)
            probs_ref[head, step * rows:(step + 1) * rows, :] = probs
            outs[step][:, lanes] = dot(probs.astype(BF), values[:, lanes]).astype(BF)


def attend_back_kernel(parts, *refs):
    pieces = refs[:parts]
    grads = refs[parts:2 * parts]
    probs_ref = refs[2 * parts]
    outs = refs[2 * parts + 1:3 * parts + 1]
    keys, values, grad_keys, grad_values = refs[3 * parts + 1:]
    rows = grads[0].shape[0]
    width = grads[0].shape[1]
    scaling = 1.0 / math.sqrt(DH)
    for step in range(parts):
        keys[step * rows:(step + 1) * rows, :] = pieces[step][rows:2 * rows, :]
        values[step * rows:(step + 1) * rows, :] = pieces[step][2 * rows:3 * rows, :]
    for head in range(width // DH):
        lanes = slice(head * DH, (head + 1) * DH)
        for step in range(parts):
            query = pieces[step][0:rows, lanes]
            grad = grads[step][:, lanes]
            probs = probs_ref[head, step * rows:(step + 1) * rows, :]
            grad_probs = dot(grad, values[:, lanes], NT)
            delta = jnp.sum(probs * grad_probs, axis=-1, keepdims=True)
            grad_scores = (probs * (grad_probs - delta) * scaling).astype(BF)
            outs[step][0:rows, lanes] = dot(grad_scores, keys[:, lanes]).astype(BF)
            key_part = dot(grad_scores, query, TN)
            value_part = dot(probs.astype(BF), grad, TN)
            if step == 0:
                grad_keys[:, lanes] = key_part
                grad_values[:, lanes] = value_part
            else:
                grad_keys[:, lanes] += key_part
                grad_values[:, lanes] += value_part
    for step in range(parts):
        outs[step][rows:2 * rows, :] = grad_keys[step * rows:(step + 1) * rows, :].astype(BF)
        outs[step][2 * rows:3 * rows, :] = grad_values[step * rows:(step + 1) * rows, :].astype(BF)


def chunk_of(array, c):
    return array[:, c * 128:(c + 1) * 128]


def lane_cat(pieces):
    return jnp.concatenate(pieces, axis=1)


def half_pickers(owners):
    shape = (owners * 4, owners * 8)
    row = lax.broadcasted_iota(jnp.int32, shape, 0)
    col = lax.broadcasted_iota(jnp.int32, shape, 1)
    first = lax.shift_left(lax.shift_right_logical(row, 2), 3) + lax.bitwise_and(row, 3)
    return [(col == first + 4 * half).astype(F32).astype(BF) for half in range(2)]


def read_tiles(ref):
    owners, lines, _ = ref.shape
    tiles = [
        ref[:, 8 * t:8 * t + 8, :].astype(F32).reshape(owners * 8, 128).astype(BF)
        for t in range(lines // 8)
    ]
    count = len(tiles) * 2 // 3
    return tiles[:count], lane_cat(tiles[count:])


def write_tiles(ref, low, high):
    owners = ref.shape[0]
    count = low.shape[1] // 128
    for c in range(count):
        ref[:, 8 * c:8 * c + 8, :] = chunk_of(low, c).reshape(owners, 8, 128).astype(BF)
    for c in range(count // 2):
        start = 8 * (count + c)
        ref[:, start:start + 8, :] = chunk_of(high, c).reshape(owners, 8, 128).astype(BF)


def split_parity(array):
    count = array.shape[1] // 128
    return [lane_cat([chunk_of(array, c) for c in range(half, count, 2)]) for half in range(2)]


def merge_parity(even, odd):
    count = even.shape[1] // 128
    return lane_cat([chunk_of(part, c) for c in range(count) for part in (even, odd)])


def unpack_rows(ref, out_ref):
    low, high = read_tiles(ref)
    owners = ref.shape[0]
    even, odd = [dot(pick, high).astype(BF) for pick in half_pickers(owners)]
    out_ref[0:owners * 8, :] = lane_cat(low)
    out_ref[owners * 8:, :] = merge_parity(even, odd)


def pack_rows(rows, ref):
    owners = ref.shape[0]
    pickers = half_pickers(owners)
    parts = split_parity(rows[owners * 8:, :].astype(BF))
    high = dot(pickers[0], parts[0], TN) + dot(pickers[1], parts[1], TN)
    write_tiles(ref, rows[0:owners * 8, :], high)


def pack_tokens(places, arrays, ref):
    low = sum([dot(place[0], x) for place, x in zip(places, arrays)])
    high = None
    for place, x in zip(places, arrays):
        for half, part in enumerate(split_parity(x)):
            term = dot(place[1 + half], part)
            high = term if high is None else high + term
    write_tiles(ref, low, high)


def unpack_tokens(place, low, high):
    even, odd = [dot(place[1 + half], high, TN) for half in range(2)]
    return dot(place[0], lane_cat(low), TN) + merge_parity(even, odd)


def column(row):
    side = row.shape[1]
    return jnp.broadcast_to(row, (side, side)).T[:, 0:1]


def place_kernel(experts, routes_ref, gates_ref, cot_ref, place_ref, packed_ref):
    tokens = cot_ref.shape[0]
    first = lax.broadcasted_iota(jnp.int32, (tokens, tokens), 0)
    second = lax.broadcasted_iota(jnp.int32, (tokens, tokens), 1)
    earlier = (first < second).astype(F32).astype(BF)
    expert_ids = lax.broadcasted_iota(jnp.int32, (experts, tokens), 0)
    line_ids = lax.broadcasted_iota(jnp.int32, (experts * 8, tokens), 0)
    routes = [routes_ref[j:j + 1, :] for j in range(TOP)]
    hits = [(route == expert_ids).astype(F32) for route in routes]
    before = dot(sum(hits[1:], hits[0]).astype(BF), earlier)
    upstream = cot_ref[...].astype(F32)
    places, arrays = [], []
    for j in range(TOP):
        rank = jnp.sum(before * hits[j], axis=0, keepdims=True).astype(jnp.int32)
        line = routes[j] * 8 + rank
        targets = (
            jnp.where(rank < 8, line, -1),
            jnp.where(rank >= 8, line - 8, -1),
            jnp.where(rank >= 8, line - 4, -1),
        )
        place = [(line_ids == target).astype(F32).astype(BF) for target in targets]
        for i, part in enumerate(place):
            place_ref[j, i] = part
        places.append(place)
        arrays.append((column(gates_ref[j:j + 1, :]) * upstream).astype(BF))
    pack_tokens(places, arrays, packed_ref)


def inverse_rms_of(attended):
    return lax.rsqrt(jnp.mean(attended * attended, axis=-1, keepdims=True) + EPSILON)


def joint_place(place_ref):
    joint = []
    for i in range(3):
        part = place_ref[0, i]
        for j in range(1, TOP):
            part = part + place_ref[j, i]
        joint.append(part)
    return joint


def norm_kernel(parts, me_ref, place_ref, *refs):
    pieces, (attended_ref, packed_ref) = refs[:parts], refs[parts:]
    me = me_ref[0]
    width = pieces[0].shape[1]
    for step in range(parts):
        attended_ref[:, lane_block(me, step, parts, width)] = pieces[step][...]
    attended = attended_ref[...].astype(F32)
    normed = (attended * inverse_rms_of(attended)).astype(BF)
    pack_tokens([joint_place(place_ref)], [normed], packed_ref)


def turn_rows(pairs, parts, rows_ref, turned_ref):
    band = rows_ref.shape[1] // (pairs * parts)
    for s in range(pairs * parts):
        block = (s % pairs) * parts + s // pairs
        turned_ref[s * band:(s + 1) * band, :] = rows_ref[:, block * band:(block + 1) * band].T


def dact_kernel(pairs, parts, packed_ref, down_ref, out_ref, turned_ref, rows):
    @pl.when(pl.program_id(0) == 0)
    def _():
        unpack_rows(packed_ref, rows)
        turn_rows(pairs, parts, rows, turned_ref)

    out_ref[...] = dot(rows[...], down_ref[...], NT)


def hidden_kernel(packed_ref, up_ref, dact_ref, hidden_ref, rows_ref):
    @pl.when(pl.program_id(0) == 0)
    def _():
        unpack_rows(packed_ref, rows_ref)

    pre = dot(rows_ref[...], up_ref[...])
    square = pre * pre
    half = 0.5 + 0.5 * jnp.tanh(pre * (GELU_COEF + (GELU_COEF * 0.044715) * square))
    act = pre * half
    hidden_ref[0] = act.astype(BF)
    slope = half + act * (1.0 - half) * (2.0 * GELU_COEF + (6.0 * GELU_COEF * 0.044715) * square)
    hidden_ref[1] = (dact_ref[...] * slope).astype(BF)


def weight_grad_kernel(pairs, parts, blocks, hidden_ref, turned_ref, rows_ref, grads_ref, turned):
    step = pl.program_id(0)

    @pl.when(step < blocks)
    def _():
        grads_ref[...] = dot(turned_ref[...], hidden_ref[0]).astype(BF)

    @pl.when(step == 0)
    def _():
        turn_rows(pairs, parts, rows_ref, turned)

    @pl.when(step >= blocks)
    def _():
        grads_ref[...] = dot(turned[...], hidden_ref[0]).astype(BF)


def project_kernel(dims, hidden_ref, weight_ref, packed_ref, total):
    step = pl.program_id(0)
    part = dot(hidden_ref[0], weight_ref[...], dims)

    @pl.when(step == 0)
    def _():
        total[...] = part

    @pl.when(step > 0)
    def _():
        total[...] += part

    @pl.when(step == pl.num_programs(0) - 1)
    def _():
        pack_rows(total[...], packed_ref)


def dattended_kernel(parts, me_ref, place_ref, back_ref, attended_ref, cot_ref, *refs):
    outs, full = refs[:parts], refs[parts]
    me = me_ref[0]
    low, high = read_tiles(back_ref)
    grad_unit = unpack_tokens(joint_place(place_ref), low, high)
    attended = attended_ref[...].astype(F32)
    inverse_rms = inverse_rms_of(attended)
    unit = attended * inverse_rms
    grad = cot_ref[...].astype(F32) + inverse_rms * (
        grad_unit - unit * jnp.mean(grad_unit * unit, axis=-1, keepdims=True)
    )
    full[...] = grad.astype(BF)
    width = outs[0].shape[1]
    for step in range(parts):
        outs[step][...] = full[:, lane_block(me, step, parts, width)]


def mix_kernel(place_ref, back_ref, attended_ref, gates_ref, out_ref):
    low, high = read_tiles(back_ref)
    mix = None
    for j in range(TOP):
        place = [place_ref[j, i] for i in range(3)]
        term = column(gates_ref[j:j + 1, :]) * unpack_tokens(place, low, high)
        mix = term if mix is None else mix + term
    out_ref[...] = (attended_ref[...].astype(F32) + mix).astype(BF)


def widen_kernel(sums_ref, up_out, down_out):
    hidden = up_out.shape[1]
    down_out[...] = sums_ref[:, 0:hidden].astype(F32).T
    up_out[...] = sums_ref[:, hidden:].astype(F32)


def shards(query, key, value, routes, gates, up, down, cotangent):
    tokens, model = query.shape[1:]
    owners = lax.axis_size("expert")
    parts = lax.axis_size("seq")
    pairs = lax.axis_size("dp")
    capacity = tokens * TOP * 3 // (2 * owners)
    slots = owners * capacity
    hidden = up.shape[2]
    width = model // parts
    length = tokens * parts
    heads = width // DH
    up, down = up[0], down[0]
    cot = cotangent[0]
    route, gate = routes[0].T, gates[0].T
    me = jnp.reshape(lax.axis_index("seq"), (1,)).astype(jnp.int32)

    def shift(piece, step):
        pairs_of = [(i, (i + step) % parts) for i in range(parts)]
        return near(lax.ppermute(piece, "seq", pairs_of))

    def swap(packed):
        return near(lax.all_to_all(packed, "expert", split_axis=0, concat_axis=0, tiled=True))

    order = (2, 1, 3) if parts == 4 else tuple(range(1, parts))

    def exchange(pieces, sign):
        moved = {step: shift(pieces[step], sign * step) for step in order}
        return [pieces[0]] + [moved[step] for step in range(1, parts)]

    triple = sds((3 * tokens, width), BF)
    single = sds((tokens, width), BF)
    wire = sds((owners, capacity * model // 128, 128), BF)
    sent = pl.pallas_call(
        functools.partial(split_kernel, parts),
        out_shape=[triple] * parts,
        in_specs=[SMEM] + [VMEM] * 3,
        out_specs=[VMEM] * parts,
        name="split_qkv",
    )(me, query[0], key[0], value[0])
    pieces = exchange(sent, 1)

    cot_late, _ = lax.optimization_barrier((cot, sent[0]))
    place, packed_grads = pl.pallas_call(
        functools.partial(place_kernel, owners),
        out_shape=[sds((TOP, 3, owners * 8, tokens), BF), wire],
        in_specs=[VMEM] * 3,
        out_specs=[VMEM] * 2,
        name="place",
    )(route, gate, cot_late)
    grad_wire = swap(packed_grads)

    attended_pieces = pl.pallas_call(
        functools.partial(attend_kernel, parts),
        out_shape=[single] * parts + [sds((heads, length, length), F32)],
        in_specs=[VMEM] * parts,
        out_specs=[VMEM] * (parts + 1),
        scratch_shapes=[pltpu.VMEM((length, width), BF)] * 2,
        compiler_params=BIG,
        cost_estimate=HEAVY,
        name="attend",
    )(*pieces)
    probs = attended_pieces[parts]
    attended_pieces = exchange(attended_pieces[:parts], -1)

    attended, packed = pl.pallas_call(
        functools.partial(norm_kernel, parts),
        out_shape=[sds((tokens, model), BF), wire],
        in_specs=[SMEM] + [VMEM] * (parts + 1),
        out_specs=[VMEM] * 2,
        name="norm_pack",
    )(me, place, *attended_pieces)
    wire_rows = swap(packed)

    blocks = 4
    chunk = hidden // blocks
    whole_wire = pl.BlockSpec(wire.shape, lambda i: (0, 0, 0))
    dact, turned = pl.pallas_call(
        functools.partial(dact_kernel, pairs, parts),
        grid=(blocks,),
        out_shape=[sds((slots, hidden), F32), sds((model, slots), BF)],
        in_specs=[VMEM, pl.BlockSpec((chunk, model), lambda i: (i, 0))],
        out_specs=[
            pl.BlockSpec((slots, chunk), lambda i: (0, i)),
            pl.BlockSpec((model, slots), lambda i: (0, 0)),
        ],
        scratch_shapes=[pltpu.VMEM((slots, model), BF)],
        compiler_params=BIG,
        name="dact",
    )(grad_wire, down)
    both, rows = pl.pallas_call(
        hidden_kernel,
        grid=(blocks,),
        out_shape=[sds((2, slots, hidden), BF), sds((slots, model), BF)],
        in_specs=[
            VMEM,
            pl.BlockSpec((model, chunk), lambda i: (0, i)),
            pl.BlockSpec((slots, chunk), lambda i: (0, i)),
        ],
        out_specs=[
            pl.BlockSpec((2, slots, chunk), lambda i: (0, 0, i)),
            pl.BlockSpec((slots, model), lambda i: (0, 0)),
        ],
        compiler_params=BIG,
        name="expert_hidden",
    )(wire_rows, up, dact)

    half = hidden // 2
    partial_grads = pl.pallas_call(
        functools.partial(weight_grad_kernel, pairs, parts, 2),
        grid=(4,),
        out_shape=sds((model, 2 * hidden), BF),
        in_specs=[
            pl.BlockSpec((1, slots, half), lambda i: (lax.div(i, 2), 0, lax.rem(i, 2))),
            pl.BlockSpec((model, slots), lambda i: (0, 0)),
            pl.BlockSpec((slots, model), lambda i: (0, 0)),
        ],
        out_specs=pl.BlockSpec((model, half), lambda i: (0, i)),
        scratch_shapes=[pltpu.VMEM((model, slots), BF)],
        compiler_params=BIG,
        name="weight_grads",
    )(both, turned, rows)
    sums = lax.psum_scatter(partial_grads, ("seq", "dp"), scatter_dimension=0, tiled=True)

    def project(source, which, weight, weight_spec, dims, cost, name):
        return pl.pallas_call(
            functools.partial(project_kernel, dims),
            grid=(blocks,),
            out_shape=wire,
            in_specs=[pl.BlockSpec((1, slots, chunk), lambda i: (which, 0, i)), weight_spec],
            out_specs=whole_wire,
            scratch_shapes=[pltpu.VMEM((slots, model), F32)],
            compiler_params=BIG,
            cost_estimate=cost,
            name=name,
        )(source, weight)

    both_late, _ = lax.optimization_barrier((both, partial_grads))
    dnormed = project(
        both_late, 1, up, pl.BlockSpec((model, chunk), lambda i: (0, i)), NT, HEAVY, "dnormed"
    )
    both_last, _ = lax.optimization_barrier((both_late, dnormed))
    dnormed_back = swap(dnormed)
    produced = project(
        both_last, 0, down, pl.BlockSpec((chunk, model), lambda i: (i, 0)), NN, None, "expert_out"
    )

    dnormed_back, produced = lax.optimization_barrier((dnormed_back, produced))
    grad_pieces = pl.pallas_call(
        functools.partial(dattended_kernel, parts),
        out_shape=[single] * parts,
        in_specs=[SMEM] + [VMEM] * 4,
        out_specs=[VMEM] * parts,
        scratch_shapes=[pltpu.VMEM((tokens, model), BF)],
        name="dattended",
    )(me, place, dnormed_back, attended, cot)
    grad_pieces = exchange(grad_pieces, 1)

    produced_back = swap(produced)

    back_pieces = pl.pallas_call(
        functools.partial(attend_back_kernel, parts),
        out_shape=[triple] * parts,
        in_specs=[VMEM] * (2 * parts + 1),
        out_specs=[VMEM] * parts,
        scratch_shapes=[pltpu.VMEM((length, width), BF)] * 2
        + [pltpu.VMEM((length, width), F32)] * 2,
        compiler_params=BIG,
        cost_estimate=MIDDLE,
        name="attend_back",
    )(*pieces, *grad_pieces, probs)
    back_pieces = exchange(back_pieces, -1)

    layer_output = pl.pallas_call(
        mix_kernel,
        out_shape=sds((tokens, model), BF),
        in_specs=[VMEM] * 4,
        out_specs=VMEM,
        name="mix",
    )(place, produced_back, attended, gate)
    grad_queries, grad_keys, grad_values = pl.pallas_call(
        functools.partial(join_kernel, parts),
        out_shape=[sds((tokens, model), BF)] * 3,
        in_specs=[SMEM] + [VMEM] * parts,
        out_specs=[VMEM] * 3,
        name="join_grads",
    )(me, *back_pieces)
    band = model // (pairs * parts)
    grad_up, grad_down = pl.pallas_call(
        widen_kernel,
        out_shape=[sds((band, hidden), F32), sds((hidden, band), F32)],
        in_specs=[VMEM],
        out_specs=[VMEM] * 2,
        name="widen",
    )(sums)
    return (
        layer_output[None],
        grad_queries[None],
        grad_keys[None],
        grad_values[None],
        grad_up[None],
        grad_down[None],
    )


def solution(mesh):
    rows = P(("dp", "expert"), "seq", None)
    weight = P("expert", None, None)
    return jax.shard_map(
        shards,
        mesh=mesh,
        in_specs=(rows, rows, rows, rows, rows, weight, weight, rows),
        out_specs=(rows, rows, rows, rows, P("expert", ("dp", "seq"), None), P("expert", None, ("dp", "seq"))),
        check_vma=False,
    )
```

```python
import functools
import math

import jax
import jax.numpy as jnp
from jax import lax
from jax.experimental import pallas as pl
from jax.experimental.pallas import tpu as pltpu
from jax.sharding import PartitionSpec as P

DH = 128
TOP = 2
EPSILON = 1e-06
GELU_COEF = math.sqrt(2.0 / math.pi)
BF = jnp.bfloat16
F32 = jnp.float32
VMEM = pl.BlockSpec(memory_space=pltpu.VMEM)
SMEM = pl.BlockSpec(memory_space=pltpu.SMEM)
NN = (((1,), (0,)), ((), ()))
NT = (((1,), (1,)), ((), ()))
TN = (((0,), (0,)), ((), ()))
HEAVY = pl.CostEstimate(flops=1_000_000_000_000, transcendentals=0, bytes_accessed=1_000_000)
MIDDLE = pl.CostEstimate(flops=40_000_000_000, transcendentals=0, bytes_accessed=1_000_000)
BIG = pltpu.CompilerParams(vmem_limit_bytes=56 * 1024 * 1024)


def dot(a, b, dims=NN):
    return lax.dot_general(a, b, dims, preferred_element_type=F32)


def sds(shape, dtype):
    return jax.ShapeDtypeStruct(shape, dtype)


def near(array):
    return pltpu.with_memory_space_constraint(array, pltpu.VMEM)


def lane_block(me, step, parts, width):
    return pl.ds(pl.multiple_of(lax.rem(me + step, parts) * width, width), width)


def split_kernel(parts, me_ref, q_ref, k_ref, v_ref, *outs):
    me = me_ref[0]
    rows = q_ref.shape[0]
    width = q_ref.shape[1] // parts
    for step in range(parts):
        lanes = lane_block(me, step, parts, width)
        for i, ref in enumerate((q_ref, k_ref, v_ref)):
            outs[step][i * rows:(i + 1) * rows, :] = ref[:, lanes]


def join_kernel(parts, me_ref, *refs):
    me = me_ref[0]
    pieces, outs = refs[:parts], refs[parts:]
    rows = outs[0].shape[0]
    width = outs[0].shape[1] // parts
    for step in range(parts):
        lanes = lane_block(me, step, parts, width)
        for i, ref in enumerate(outs):
            ref[:, lanes] = pieces[step][i * rows:(i + 1) * rows, :]


def attend_kernel(parts, *refs):
    pieces = refs[:parts]
    outs = refs[parts:2 * parts]
    probs_ref, keys, values = refs[2 * parts:]
    rows = outs[0].shape[0]
    width = outs[0].shape[1]
    scaling = 1.0 / math.sqrt(DH)
    for step in range(parts):
        keys[step * rows:(step + 1) * rows, :] = pieces[step][rows:2 * rows, :]
        values[step * rows:(step + 1) * rows, :] = pieces[step][2 * rows:3 * rows, :]
    for head in range(width // DH):
        lanes = slice(head * DH, (head + 1) * DH)
        for step in range(parts):
            scores = dot(pieces[step][0:rows, lanes], keys[:, lanes], NT) * scaling
            exponent = jnp.exp(scores - jnp.max(scores, axis=-1, keepdims=True))
            probs = exponent / jnp.sum(exponent, axis=-1, keepdims=True)
            probs_ref[head, step * rows:(step + 1) * rows, :] = probs
            outs[step][:, lanes] = dot(probs.astype(BF), values[:, lanes]).astype(BF)


def attend_back_kernel(parts, *refs):
    pieces = refs[:parts]
    grads = refs[parts:2 * parts]
    probs_ref = refs[2 * parts]
    outs = refs[2 * parts + 1:3 * parts + 1]
    keys, values, grad_keys, grad_values = refs[3 * parts + 1:]
    rows = grads[0].shape[0]
    width = grads[0].shape[1]
    scaling = 1.0 / math.sqrt(DH)
    for step in range(parts):
        keys[step * rows:(step + 1) * rows, :] = pieces[step][rows:2 * rows, :]
        values[step * rows:(step + 1) * rows, :] = pieces[step][2 * rows:3 * rows, :]
    for head in range(width // DH):
        lanes = slice(head * DH, (head + 1) * DH)
        for step in range(parts):
            query = pieces[step][0:rows, lanes]
            grad = grads[step][:, lanes]
            probs = probs_ref[head, step * rows:(step + 1) * rows, :]
            grad_probs = dot(grad, values[:, lanes], NT)
            delta = jnp.sum(probs * grad_probs, axis=-1, keepdims=True)
            grad_scores = (probs * (grad_probs - delta) * scaling).astype(BF)
            outs[step][0:rows, lanes] = dot(grad_scores, keys[:, lanes]).astype(BF)
            key_part = dot(grad_scores, query, TN)
            value_part = dot(probs.astype(BF), grad, TN)
            if step == 0:
                grad_keys[:, lanes] = key_part
                grad_values[:, lanes] = value_part
            else:
                grad_keys[:, lanes] += key_part
                grad_values[:, lanes] += value_part
    for step in range(parts):
        outs[step][rows:2 * rows, :] = grad_keys[step * rows:(step + 1) * rows, :].astype(BF)
        outs[step][2 * rows:3 * rows, :] = grad_values[step * rows:(step + 1) * rows, :].astype(BF)


def chunk_of(array, c):
    return array[:, c * 128:(c + 1) * 128]


def lane_cat(pieces):
    return jnp.concatenate(pieces, axis=1)


def half_pickers(owners):
    shape = (owners * 4, owners * 8)
    row = lax.broadcasted_iota(jnp.int32, shape, 0)
    col = lax.broadcasted_iota(jnp.int32, shape, 1)
    first = lax.shift_left(lax.shift_right_logical(row, 2), 3) + lax.bitwise_and(row, 3)
    return [(col == first + 4 * half).astype(F32).astype(BF) for half in range(2)]


def read_tiles(ref):
    owners, lines, _ = ref.shape
    tiles = [
        ref[:, 8 * t:8 * t + 8, :].astype(F32).reshape(owners * 8, 128).astype(BF)
        for t in range(lines // 8)
    ]
    count = len(tiles) * 2 // 3
    return tiles[:count], lane_cat(tiles[count:])


def write_tiles(ref, low, high):
    owners = ref.shape[0]
    count = low.shape[1] // 128
    for c in range(count):
        ref[:, 8 * c:8 * c + 8, :] = chunk_of(low, c).reshape(owners, 8, 128).astype(BF)
    for c in range(count // 2):
        start = 8 * (count + c)
        ref[:, start:start + 8, :] = chunk_of(high, c).reshape(owners, 8, 128).astype(BF)


def split_parity(array):
    count = array.shape[1] // 128
    return [lane_cat([chunk_of(array, c) for c in range(half, count, 2)]) for half in range(2)]


def merge_parity(even, odd):
    count = even.shape[1] // 128
    return lane_cat([chunk_of(part, c) for c in range(count) for part in (even, odd)])


def unpack_rows(ref, out_ref):
    low, high = read_tiles(ref)
    owners = ref.shape[0]
    even, odd = [dot(pick, high).astype(BF) for pick in half_pickers(owners)]
    out_ref[0:owners * 8, :] = lane_cat(low)
    out_ref[owners * 8:, :] = merge_parity(even, odd)


def pack_rows(rows, ref):
    owners = ref.shape[0]
    pickers = half_pickers(owners)
    parts = split_parity(rows[owners * 8:, :].astype(BF))
    high = dot(pickers[0], parts[0], TN) + dot(pickers[1], parts[1], TN)
    write_tiles(ref, rows[0:owners * 8, :], high)


def pack_tokens(places, arrays, ref):
    low = sum([dot(place[0], x) for place, x in zip(places, arrays)])
    high = None
    for place, x in zip(places, arrays):
        for half, part in enumerate(split_parity(x)):
            term = dot(place[1 + half], part)
            high = term if high is None else high + term
    write_tiles(ref, low, high)


def unpack_tokens(place, low, high):
    even, odd = [dot(place[1 + half], high, TN) for half in range(2)]
    return dot(place[0], lane_cat(low), TN) + merge_parity(even, odd)


def column(row):
    side = row.shape[1]
    return jnp.broadcast_to(row, (side, side)).T[:, 0:1]


def place_kernel(experts, routes_ref, gates_ref, cot_ref, place_ref, packed_ref):
    tokens = cot_ref.shape[0]
    first = lax.broadcasted_iota(jnp.int32, (tokens, tokens), 0)
    second = lax.broadcasted_iota(jnp.int32, (tokens, tokens), 1)
    earlier = (first < second).astype(F32).astype(BF)
    expert_ids = lax.broadcasted_iota(jnp.int32, (experts, tokens), 0)
    line_ids = lax.broadcasted_iota(jnp.int32, (experts * 8, tokens), 0)
    routes = [routes_ref[j:j + 1, :] for j in range(TOP)]
    hits = [(route == expert_ids).astype(F32) for route in routes]
    before = dot(sum(hits[1:], hits[0]).astype(BF), earlier)
    upstream = cot_ref[...].astype(F32)
    places, arrays = [], []
    for j in range(TOP):
        rank = jnp.sum(before * hits[j], axis=0, keepdims=True).astype(jnp.int32)
        line = routes[j] * 8 + rank
        targets = (
            jnp.where(rank < 8, line, -1),
            jnp.where(rank >= 8, line - 8, -1),
            jnp.where(rank >= 8, line - 4, -1),
        )
        place = [(line_ids == target).astype(F32).astype(BF) for target in targets]
        for i, part in enumerate(place):
            place_ref[j, i] = part
        places.append(place)
        arrays.append((column(gates_ref[j:j + 1, :]) * upstream).astype(BF))
    pack_tokens(places, arrays, packed_ref)


def inverse_rms_of(attended):
    return lax.rsqrt(jnp.mean(attended * attended, axis=-1, keepdims=True) + EPSILON)


def joint_place(place_ref):
    joint = []
    for i in range(3):
        part = place_ref[0, i]
        for j in range(1, TOP):
            part = part + place_ref[j, i]
        joint.append(part)
    return joint


def norm_kernel(parts, me_ref, place_ref, *refs):
    pieces, (attended_ref, packed_ref) = refs[:parts], refs[parts:]
    me = me_ref[0]
    width = pieces[0].shape[1]
    for step in range(parts):
        attended_ref[:, lane_block(me, step, parts, width)] = pieces[step][...]
    attended = attended_ref[...].astype(F32)
    normed = (attended * inverse_rms_of(attended)).astype(BF)
    pack_tokens([joint_place(place_ref)], [normed], packed_ref)


def turn_rows(pairs, parts, rows_ref, turned_ref):
    band = rows_ref.shape[1] // (pairs * parts)
    for s in range(pairs * parts):
        block = (s % pairs) * parts + s // pairs
        turned_ref[s * band:(s + 1) * band, :] = rows_ref[:, block * band:(block + 1) * band].T


def dact_kernel(pairs, parts, packed_ref, down_ref, out_ref, turned_ref, rows):
    @pl.when(pl.program_id(0) == 0)
    def _():
        unpack_rows(packed_ref, rows)
        turn_rows(pairs, parts, rows, turned_ref)

    out_ref[...] = dot(rows[...], down_ref[...], NT)


def expert_kernel(packed_ref, up_ref, dact_ref, hidden_ref, rows_ref, dnormed_ref, total):
    step = pl.program_id(0)

    @pl.when(step == 0)
    def _():
        unpack_rows(packed_ref, rows_ref)

    pre = dot(rows_ref[...], up_ref[...])
    square = pre * pre
    half = 0.5 + 0.5 * jnp.tanh(pre * (GELU_COEF + (GELU_COEF * 0.044715) * square))
    act = pre * half
    hidden_ref[0] = act.astype(BF)
    slope = half + act * (1.0 - half) * (2.0 * GELU_COEF + (6.0 * GELU_COEF * 0.044715) * square)
    dpre = (dact_ref[...] * slope).astype(BF)
    hidden_ref[1] = dpre
    part = dot(dpre, up_ref[...], NT)

    @pl.when(step == 0)
    def _():
        total[...] = part

    @pl.when(step > 0)
    def _():
        total[...] += part

    @pl.when(step == pl.num_programs(0) - 1)
    def _():
        pack_rows(total[...], dnormed_ref)


def weight_grad_kernel(pairs, parts, blocks, hidden_ref, turned_ref, rows_ref, grads_ref, turned):
    step = pl.program_id(0)

    @pl.when(step < blocks)
    def _():
        grads_ref[...] = dot(turned_ref[...], hidden_ref[0]).astype(BF)

    @pl.when(step == 0)
    def _():
        turn_rows(pairs, parts, rows_ref, turned)

    @pl.when(step >= blocks)
    def _():
        grads_ref[...] = dot(turned[...], hidden_ref[0]).astype(BF)


def out_kernel(hidden_ref, weight_ref, packed_ref, total):
    step = pl.program_id(0)
    part = dot(hidden_ref[0], weight_ref[...])

    @pl.when(step == 0)
    def _():
        total[...] = part

    @pl.when(step > 0)
    def _():
        total[...] += part

    @pl.when(step == pl.num_programs(0) - 1)
    def _():
        pack_rows(total[...], packed_ref)


def dattended_kernel(parts, me_ref, place_ref, back_ref, attended_ref, cot_ref, *refs):
    outs, full = refs[:parts], refs[parts]
    me = me_ref[0]
    low, high = read_tiles(back_ref)
    grad_unit = unpack_tokens(joint_place(place_ref), low, high)
    attended = attended_ref[...].astype(F32)
    inverse_rms = inverse_rms_of(attended)
    unit = attended * inverse_rms
    grad = cot_ref[...].astype(F32) + inverse_rms * (
        grad_unit - unit * jnp.mean(grad_unit * unit, axis=-1, keepdims=True)
    )
    full[...] = grad.astype(BF)
    width = outs[0].shape[1]
    for step in range(parts):
        outs[step][...] = full[:, lane_block(me, step, parts, width)]


def mix_kernel(place_ref, back_ref, attended_ref, gates_ref, out_ref):
    low, high = read_tiles(back_ref)
    mix = None
    for j in range(TOP):
        place = [place_ref[j, i] for i in range(3)]
        term = column(gates_ref[j:j + 1, :]) * unpack_tokens(place, low, high)
        mix = term if mix is None else mix + term
    out_ref[...] = (attended_ref[...].astype(F32) + mix).astype(BF)


def widen_kernel(sums_ref, up_out, down_out):
    hidden = up_out.shape[1]
    down_out[...] = sums_ref[:, 0:hidden].astype(F32).T
    up_out[...] = sums_ref[:, hidden:].astype(F32)


def shards(query, key, value, routes, gates, up, down, cotangent):
    tokens, model = query.shape[1:]
    owners = lax.axis_size("expert")
    parts = lax.axis_size("seq")
    pairs = lax.axis_size("dp")
    capacity = tokens * TOP * 3 // (2 * owners)
    slots = owners * capacity
    hidden = up.shape[2]
    width = model // parts
    length = tokens * parts
    heads = width // DH
    up, down = up[0], down[0]
    cot = cotangent[0]
    route, gate = routes[0].T, gates[0].T
    me = jnp.reshape(lax.axis_index("seq"), (1,)).astype(jnp.int32)

    def shift(piece, step):
        pairs_of = [(i, (i + step) % parts) for i in range(parts)]
        return near(lax.ppermute(piece, "seq", pairs_of))

    def swap(packed):
        return near(lax.all_to_all(packed, "expert", split_axis=0, concat_axis=0, tiled=True))

    order = (2, 1, 3) if parts == 4 else tuple(range(1, parts))

    def exchange(pieces, sign):
        moved = {step: shift(pieces[step], sign * step) for step in order}
        return [pieces[0]] + [moved[step] for step in range(1, parts)]

    triple = sds((3 * tokens, width), BF)
    single = sds((tokens, width), BF)
    wire = sds((owners, capacity * model // 128, 128), BF)
    sent = pl.pallas_call(
        functools.partial(split_kernel, parts),
        out_shape=[triple] * parts,
        in_specs=[SMEM] + [VMEM] * 3,
        out_specs=[VMEM] * parts,
        name="split_qkv",
    )(me, query[0], key[0], value[0])
    pieces = exchange(sent, 1)

    cot_late, _ = lax.optimization_barrier((cot, sent[0]))
    place, packed_grads = pl.pallas_call(
        functools.partial(place_kernel, owners),
        out_shape=[sds((TOP, 3, owners * 8, tokens), BF), wire],
        in_specs=[VMEM] * 3,
        out_specs=[VMEM] * 2,
        name="place",
    )(route, gate, cot_late)
    grad_wire = swap(packed_grads)

    attended_pieces = pl.pallas_call(
        functools.partial(attend_kernel, parts),
        out_shape=[single] * parts + [sds((heads, length, length), F32)],
        in_specs=[VMEM] * parts,
        out_specs=[VMEM] * (parts + 1),
        scratch_shapes=[pltpu.VMEM((length, width), BF)] * 2,
        compiler_params=BIG,
        cost_estimate=HEAVY,
        name="attend",
    )(*pieces)
    probs = attended_pieces[parts]
    attended_pieces = exchange(attended_pieces[:parts], -1)

    attended, packed = pl.pallas_call(
        functools.partial(norm_kernel, parts),
        out_shape=[sds((tokens, model), BF), wire],
        in_specs=[SMEM] + [VMEM] * (parts + 1),
        out_specs=[VMEM] * 2,
        name="norm_pack",
    )(me, place, *attended_pieces)
    wire_rows = swap(packed)

    blocks = 4
    chunk = hidden // blocks
    whole_wire = pl.BlockSpec(wire.shape, lambda i: (0, 0, 0))
    dact, turned = pl.pallas_call(
        functools.partial(dact_kernel, pairs, parts),
        grid=(blocks,),
        out_shape=[sds((slots, hidden), F32), sds((model, slots), BF)],
        in_specs=[VMEM, pl.BlockSpec((chunk, model), lambda i: (i, 0))],
        out_specs=[
            pl.BlockSpec((slots, chunk), lambda i: (0, i)),
            pl.BlockSpec((model, slots), lambda i: (0, 0)),
        ],
        scratch_shapes=[pltpu.VMEM((slots, model), BF)],
        compiler_params=BIG,
        name="dact",
    )(grad_wire, down)
    both, rows, dnormed = pl.pallas_call(
        expert_kernel,
        grid=(blocks,),
        out_shape=[sds((2, slots, hidden), BF), sds((slots, model), BF), wire],
        in_specs=[
            VMEM,
            pl.BlockSpec((model, chunk), lambda i: (0, i)),
            pl.BlockSpec((slots, chunk), lambda i: (0, i)),
        ],
        out_specs=[
            pl.BlockSpec((2, slots, chunk), lambda i: (0, 0, i)),
            pl.BlockSpec((slots, model), lambda i: (0, 0)),
            whole_wire,
        ],
        scratch_shapes=[pltpu.VMEM((slots, model), F32)],
        compiler_params=BIG,
        name="expert",
    )(wire_rows, up, dact)
    dnormed_back = swap(dnormed)

    half = hidden // 2
    partial_grads = pl.pallas_call(
        functools.partial(weight_grad_kernel, pairs, parts, 2),
        grid=(4,),
        out_shape=sds((model, 2 * hidden), BF),
        in_specs=[
            pl.BlockSpec((1, slots, half), lambda i: (lax.div(i, 2), 0, lax.rem(i, 2))),
            pl.BlockSpec((model, slots), lambda i: (0, 0)),
            pl.BlockSpec((slots, model), lambda i: (0, 0)),
        ],
        out_specs=pl.BlockSpec((model, half), lambda i: (0, i)),
        scratch_shapes=[pltpu.VMEM((model, slots), BF)],
        compiler_params=BIG,
        name="weight_grads",
    )(both, turned, rows)
    sums = lax.psum_scatter(partial_grads, ("seq", "dp"), scatter_dimension=0, tiled=True)

    both_late, _ = lax.optimization_barrier((both, partial_grads))
    produced = pl.pallas_call(
        out_kernel,
        grid=(blocks,),
        out_shape=wire,
        in_specs=[
            pl.BlockSpec((1, slots, chunk), lambda i: (0, 0, i)),
            pl.BlockSpec((chunk, model), lambda i: (i, 0)),
        ],
        out_specs=whole_wire,
        scratch_shapes=[pltpu.VMEM((slots, model), F32)],
        compiler_params=BIG,
        name="expert_out",
    )(both_late, down)

    dnormed_back, produced = lax.optimization_barrier((dnormed_back, produced))
    grad_pieces = pl.pallas_call(
        functools.partial(dattended_kernel, parts),
        out_shape=[single] * parts,
        in_specs=[SMEM] + [VMEM] * 4,
        out_specs=[VMEM] * parts,
        scratch_shapes=[pltpu.VMEM((tokens, model), BF)],
        cost_estimate=HEAVY,
        name="dattended",
    )(me, place, dnormed_back, attended, cot)
    grad_pieces = exchange(grad_pieces, 1)

    produced_back = swap(produced)

    back_pieces = pl.pallas_call(
        functools.partial(attend_back_kernel, parts),
        out_shape=[triple] * parts,
        in_specs=[VMEM] * (2 * parts + 1),
        out_specs=[VMEM] * parts,
        scratch_shapes=[pltpu.VMEM((length, width), BF)] * 2
        + [pltpu.VMEM((length, width), F32)] * 2,
        compiler_params=BIG,
        cost_estimate=MIDDLE,
        name="attend_back",
    )(*pieces, *grad_pieces, probs)
    back_pieces = exchange(back_pieces, -1)

    layer_output = pl.pallas_call(
        mix_kernel,
        out_shape=sds((tokens, model), BF),
        in_specs=[VMEM] * 4,
        out_specs=VMEM,
        name="mix",
    )(place, produced_back, attended, gate)
    grad_queries, grad_keys, grad_values = pl.pallas_call(
        functools.partial(join_kernel, parts),
        out_shape=[sds((tokens, model), BF)] * 3,
        in_specs=[SMEM] + [VMEM] * parts,
        out_specs=[VMEM] * 3,
        name="join_grads",
    )(me, *back_pieces)
    band = model // (pairs * parts)
    grad_up, grad_down = pl.pallas_call(
        widen_kernel,
        out_shape=[sds((band, hidden), F32), sds((hidden, band), F32)],
        in_specs=[VMEM],
        out_specs=[VMEM] * 2,
        name="widen",
    )(sums)
    return (
        layer_output[None],
        grad_queries[None],
        grad_keys[None],
        grad_values[None],
        grad_up[None],
        grad_down[None],
    )


def solution(mesh):
    rows = P(("dp", "expert"), "seq", None)
    weight = P("expert", None, None)
    return jax.shard_map(
        shards,
        mesh=mesh,
        in_specs=(rows, rows, rows, rows, rows, weight, weight, rows),
        out_specs=(rows, rows, rows, rows, P("expert", ("dp", "seq"), None), P("expert", None, ("dp", "seq"))),
        check_vma=False,
    )
```

```python
import functools
import math

import jax
import jax.numpy as jnp
from jax import lax
from jax.experimental import pallas as pl
from jax.experimental.pallas import tpu as pltpu
from jax.sharding import PartitionSpec as P

DH = 128
TOP = 2
EPSILON = 1e-06
GELU_COEF = math.sqrt(2.0 / math.pi)
BF = jnp.bfloat16
F32 = jnp.float32
VMEM = pl.BlockSpec(memory_space=pltpu.VMEM)
SMEM = pl.BlockSpec(memory_space=pltpu.SMEM)
NN = (((1,), (0,)), ((), ()))
NT = (((1,), (1,)), ((), ()))
TN = (((0,), (0,)), ((), ()))
HEAVY = pl.CostEstimate(flops=1_000_000_000_000, transcendentals=0, bytes_accessed=1_000_000)
MIDDLE = pl.CostEstimate(flops=40_000_000_000, transcendentals=0, bytes_accessed=1_000_000)
BIG = pltpu.CompilerParams(vmem_limit_bytes=56 * 1024 * 1024)


def dot(a, b, dims=NN):
    return lax.dot_general(a, b, dims, preferred_element_type=F32)


def sds(shape, dtype):
    return jax.ShapeDtypeStruct(shape, dtype)


def near(array):
    return pltpu.with_memory_space_constraint(array, pltpu.VMEM)


def lane_block(me, step, parts, width):
    return pl.ds(pl.multiple_of(lax.rem(me + step, parts) * width, width), width)


def split_kernel(parts, me_ref, q_ref, k_ref, v_ref, *outs):
    me = me_ref[0]
    rows = q_ref.shape[0]
    width = q_ref.shape[1] // parts
    for step in range(parts):
        lanes = lane_block(me, step, parts, width)
        for i, ref in enumerate((q_ref, k_ref, v_ref)):
            outs[step][i * rows:(i + 1) * rows, :] = ref[:, lanes]


def join_kernel(parts, me_ref, *refs):
    me = me_ref[0]
    pieces, outs = refs[:parts], refs[parts:]
    rows = outs[0].shape[0]
    width = outs[0].shape[1] // parts
    for step in range(parts):
        lanes = lane_block(me, step, parts, width)
        for i, ref in enumerate(outs):
            ref[:, lanes] = pieces[step][i * rows:(i + 1) * rows, :]


def attend_kernel(parts, *refs):
    pieces = refs[:parts]
    outs = refs[parts:2 * parts]
    probs_ref, keys, values = refs[2 * parts:]
    rows = outs[0].shape[0]
    width = outs[0].shape[1]
    scaling = 1.0 / math.sqrt(DH)
    for step in range(parts):
        keys[step * rows:(step + 1) * rows, :] = pieces[step][rows:2 * rows, :]
        values[step * rows:(step + 1) * rows, :] = pieces[step][2 * rows:3 * rows, :]
    for head in range(width // DH):
        lanes = slice(head * DH, (head + 1) * DH)
        for step in range(parts):
            scores = dot(pieces[step][0:rows, lanes], keys[:, lanes], NT) * scaling
            exponent = jnp.exp(scores - jnp.max(scores, axis=-1, keepdims=True))
            probs = exponent / jnp.sum(exponent, axis=-1, keepdims=True)
            rounded = probs.astype(BF)
            probs_ref[head, step * rows:(step + 1) * rows, :] = rounded
            outs[step][:, lanes] = dot(rounded, values[:, lanes]).astype(BF)


def attend_back_kernel(parts, *refs):
    pieces = refs[:parts]
    grads = refs[parts:2 * parts]
    probs_ref = refs[2 * parts]
    outs = refs[2 * parts + 1:3 * parts + 1]
    keys, values, grad_keys, grad_values = refs[3 * parts + 1:]
    rows = grads[0].shape[0]
    width = grads[0].shape[1]
    scaling = 1.0 / math.sqrt(DH)
    for step in range(parts):
        keys[step * rows:(step + 1) * rows, :] = pieces[step][rows:2 * rows, :]
        values[step * rows:(step + 1) * rows, :] = pieces[step][2 * rows:3 * rows, :]
    for head in range(width // DH):
        lanes = slice(head * DH, (head + 1) * DH)
        for step in range(parts):
            query = pieces[step][0:rows, lanes]
            grad = grads[step][:, lanes]
            rounded = probs_ref[head, step * rows:(step + 1) * rows, :]
            probs = rounded.astype(F32)
            grad_probs = dot(grad, values[:, lanes], NT)
            delta = jnp.sum(probs * grad_probs, axis=-1, keepdims=True)
            grad_scores = (probs * (grad_probs - delta) * scaling).astype(BF)
            outs[step][0:rows, lanes] = dot(grad_scores, keys[:, lanes]).astype(BF)
            key_part = dot(grad_scores, query, TN)
            value_part = dot(rounded, grad, TN)
            if step == 0:
                grad_keys[:, lanes] = key_part
                grad_values[:, lanes] = value_part
            else:
                grad_keys[:, lanes] += key_part
                grad_values[:, lanes] += value_part
    for step in range(parts):
        outs[step][rows:2 * rows, :] = grad_keys[step * rows:(step + 1) * rows, :].astype(BF)
        outs[step][2 * rows:3 * rows, :] = grad_values[step * rows:(step + 1) * rows, :].astype(BF)


def chunk_of(array, c):
    return array[:, c * 128:(c + 1) * 128]


def lane_cat(pieces):
    return jnp.concatenate(pieces, axis=1)


def half_pickers(owners):
    shape = (owners * 4, owners * 8)
    row = lax.broadcasted_iota(jnp.int32, shape, 0)
    col = lax.broadcasted_iota(jnp.int32, shape, 1)
    first = lax.shift_left(lax.shift_right_logical(row, 2), 3) + lax.bitwise_and(row, 3)
    return [(col == first + 4 * half).astype(F32).astype(BF) for half in range(2)]


def read_tiles(ref):
    owners, lines, _ = ref.shape
    tiles = [
        ref[:, 8 * t:8 * t + 8, :].astype(F32).reshape(owners * 8, 128).astype(BF)
        for t in range(lines // 8)
    ]
    count = len(tiles) * 2 // 3
    return tiles[:count], lane_cat(tiles[count:])


def write_tiles(ref, low, high):
    owners = ref.shape[0]
    count = low.shape[1] // 128
    for c in range(count):
        ref[:, 8 * c:8 * c + 8, :] = chunk_of(low, c).reshape(owners, 8, 128).astype(BF)
    for c in range(count // 2):
        start = 8 * (count + c)
        ref[:, start:start + 8, :] = chunk_of(high, c).reshape(owners, 8, 128).astype(BF)


def split_parity(array):
    count = array.shape[1] // 128
    return [lane_cat([chunk_of(array, c) for c in range(half, count, 2)]) for half in range(2)]


def merge_parity(even, odd):
    count = even.shape[1] // 128
    return lane_cat([chunk_of(part, c) for c in range(count) for part in (even, odd)])


def unpack_rows(ref, out_ref):
    low, high = read_tiles(ref)
    owners = ref.shape[0]
    even, odd = [dot(pick, high).astype(BF) for pick in half_pickers(owners)]
    out_ref[0:owners * 8, :] = lane_cat(low)
    out_ref[owners * 8:, :] = merge_parity(even, odd)


def pack_rows(rows, ref):
    owners = ref.shape[0]
    pickers = half_pickers(owners)
    parts = split_parity(rows[owners * 8:, :].astype(BF))
    high = dot(pickers[0], parts[0], TN) + dot(pickers[1], parts[1], TN)
    write_tiles(ref, rows[0:owners * 8, :], high)


def pack_tokens(places, arrays, ref):
    low = sum([dot(place[0], x) for place, x in zip(places, arrays)])
    high = None
    for place, x in zip(places, arrays):
        for half, part in enumerate(split_parity(x)):
            term = dot(place[1 + half], part)
            high = term if high is None else high + term
    write_tiles(ref, low, high)


def unpack_tokens(place, low, high):
    even, odd = [dot(place[1 + half], high, TN) for half in range(2)]
    return dot(place[0], lane_cat(low), TN) + merge_parity(even, odd)


def column(row):
    side = row.shape[1]
    return jnp.broadcast_to(row, (side, side)).T[:, 0:1]


def place_kernel(experts, routes_ref, gates_ref, cot_ref, place_ref, packed_ref):
    tokens = cot_ref.shape[0]
    first = lax.broadcasted_iota(jnp.int32, (tokens, tokens), 0)
    second = lax.broadcasted_iota(jnp.int32, (tokens, tokens), 1)
    earlier = (first < second).astype(F32).astype(BF)
    expert_ids = lax.broadcasted_iota(jnp.int32, (experts, tokens), 0)
    line_ids = lax.broadcasted_iota(jnp.int32, (experts * 8, tokens), 0)
    routes = [routes_ref[j:j + 1, :] for j in range(TOP)]
    hits = [(route == expert_ids).astype(F32) for route in routes]
    before = dot(sum(hits[1:], hits[0]).astype(BF), earlier)
    upstream = cot_ref[...].astype(F32)
    places, arrays = [], []
    for j in range(TOP):
        rank = jnp.sum(before * hits[j], axis=0, keepdims=True).astype(jnp.int32)
        line = routes[j] * 8 + rank
        targets = (
            jnp.where(rank < 8, line, -1),
            jnp.where(rank >= 8, line - 8, -1),
            jnp.where(rank >= 8, line - 4, -1),
        )
        place = [(line_ids == target).astype(F32).astype(BF) for target in targets]
        for i, part in enumerate(place):
            place_ref[j, i] = part
        places.append(place)
        arrays.append((column(gates_ref[j:j + 1, :]) * upstream).astype(BF))
    pack_tokens(places, arrays, packed_ref)


def inverse_rms_of(attended):
    return lax.rsqrt(jnp.mean(attended * attended, axis=-1, keepdims=True) + EPSILON)


def joint_place(place_ref):
    joint = []
    for i in range(3):
        part = place_ref[0, i]
        for j in range(1, TOP):
            part = part + place_ref[j, i]
        joint.append(part)
    return joint


def norm_kernel(parts, me_ref, place_ref, *refs):
    pieces, (attended_ref, packed_ref) = refs[:parts], refs[parts:]
    me = me_ref[0]
    width = pieces[0].shape[1]
    for step in range(parts):
        attended_ref[:, lane_block(me, step, parts, width)] = pieces[step][...]
    attended = attended_ref[...].astype(F32)
    normed = (attended * inverse_rms_of(attended)).astype(BF)
    pack_tokens([joint_place(place_ref)], [normed], packed_ref)


def turn_rows(pairs, parts, rows_ref, turned_ref):
    band = rows_ref.shape[1] // (pairs * parts)
    for s in range(pairs * parts):
        block = (s % pairs) * parts + s // pairs
        turned_ref[s * band:(s + 1) * band, :] = rows_ref[:, block * band:(block + 1) * band].T


def dact_kernel(pairs, parts, packed_ref, down_ref, out_ref, turned_ref, rows):
    @pl.when(pl.program_id(0) == 0)
    def _():
        unpack_rows(packed_ref, rows)
        turn_rows(pairs, parts, rows, turned_ref)

    out_ref[...] = dot(rows[...], down_ref[...], NT)


def expert_kernel(packed_ref, up_ref, dact_ref, hidden_ref, rows_ref, dnormed_ref, total):
    step = pl.program_id(0)

    @pl.when(step == 0)
    def _():
        unpack_rows(packed_ref, rows_ref)

    pre = dot(rows_ref[...], up_ref[...])
    square = pre * pre
    half = 0.5 + 0.5 * jnp.tanh(pre * (GELU_COEF + (GELU_COEF * 0.044715) * square))
    act = pre * half
    hidden_ref[0] = act.astype(BF)
    slope = half + act * (1.0 - half) * (2.0 * GELU_COEF + (6.0 * GELU_COEF * 0.044715) * square)
    dpre = (dact_ref[...] * slope).astype(BF)
    hidden_ref[1] = dpre
    part = dot(dpre, up_ref[...], NT)

    @pl.when(step == 0)
    def _():
        total[...] = part

    @pl.when(step > 0)
    def _():
        total[...] += part

    @pl.when(step == pl.num_programs(0) - 1)
    def _():
        pack_rows(total[...], dnormed_ref)


def weight_grad_kernel(pairs, parts, blocks, hidden_ref, turned_ref, rows_ref, grads_ref, turned):
    step = pl.program_id(0)

    @pl.when(step < blocks)
    def _():
        grads_ref[...] = dot(turned_ref[...], hidden_ref[0]).astype(BF)

    @pl.when(step == 0)
    def _():
        turn_rows(pairs, parts, rows_ref, turned)

    @pl.when(step >= blocks)
    def _():
        grads_ref[...] = dot(turned[...], hidden_ref[0]).astype(BF)


def out_kernel(hidden_ref, weight_ref, packed_ref, total):
    step = pl.program_id(0)
    part = dot(hidden_ref[0], weight_ref[...])

    @pl.when(step == 0)
    def _():
        total[...] = part

    @pl.when(step > 0)
    def _():
        total[...] += part

    @pl.when(step == pl.num_programs(0) - 1)
    def _():
        pack_rows(total[...], packed_ref)


def dattended_kernel(parts, me_ref, place_ref, back_ref, attended_ref, cot_ref, *refs):
    outs, full = refs[:parts], refs[parts]
    me = me_ref[0]
    low, high = read_tiles(back_ref)
    grad_unit = unpack_tokens(joint_place(place_ref), low, high)
    attended = attended_ref[...].astype(F32)
    inverse_rms = inverse_rms_of(attended)
    unit = attended * inverse_rms
    grad = cot_ref[...].astype(F32) + inverse_rms * (
        grad_unit - unit * jnp.mean(grad_unit * unit, axis=-1, keepdims=True)
    )
    full[...] = grad.astype(BF)
    width = outs[0].shape[1]
    for step in range(parts):
        outs[step][...] = full[:, lane_block(me, step, parts, width)]


def mix_kernel(place_ref, back_ref, attended_ref, gates_ref, out_ref):
    low, high = read_tiles(back_ref)
    mix = None
    for j in range(TOP):
        place = [place_ref[j, i] for i in range(3)]
        term = column(gates_ref[j:j + 1, :]) * unpack_tokens(place, low, high)
        mix = term if mix is None else mix + term
    out_ref[...] = (attended_ref[...].astype(F32) + mix).astype(BF)


def widen_kernel(sums_ref, up_out, down_out):
    hidden = up_out.shape[1]
    down_out[...] = sums_ref[:, 0:hidden].astype(F32).T
    up_out[...] = sums_ref[:, hidden:].astype(F32)


def finish_kernel(parts, me_ref, sums_ref, place_ref, back_ref, attended_ref, gates_ref, *refs):
    pieces, outs = refs[:parts], refs[parts:]
    widen_kernel(sums_ref, *outs[4:])
    mix_kernel(place_ref, back_ref, attended_ref, gates_ref, outs[0])
    join_kernel(parts, me_ref, *pieces, *outs[1:4])


def shards(query, key, value, routes, gates, up, down, cotangent):
    tokens, model = query.shape[1:]
    owners = lax.axis_size("expert")
    parts = lax.axis_size("seq")
    pairs = lax.axis_size("dp")
    capacity = tokens * TOP * 3 // (2 * owners)
    slots = owners * capacity
    hidden = up.shape[2]
    width = model // parts
    length = tokens * parts
    heads = width // DH
    up, down = up[0], down[0]
    cot = cotangent[0]
    route, gate = routes[0].T, gates[0].T
    me = jnp.reshape(lax.axis_index("seq"), (1,)).astype(jnp.int32)

    def shift(piece, step):
        pairs_of = [(i, (i + step) % parts) for i in range(parts)]
        return near(lax.ppermute(piece, "seq", pairs_of))

    def swap(packed):
        return near(lax.all_to_all(packed, "expert", split_axis=0, concat_axis=0, tiled=True))

    order = (2, 1, 3) if parts == 4 else tuple(range(1, parts))

    def exchange(pieces, sign):
        moved = {step: shift(pieces[step], sign * step) for step in order}
        return [pieces[0]] + [moved[step] for step in range(1, parts)]

    triple = sds((3 * tokens, width), BF)
    single = sds((tokens, width), BF)
    wire = sds((owners, capacity * model // 128, 128), BF)
    sent = pl.pallas_call(
        functools.partial(split_kernel, parts),
        out_shape=[triple] * parts,
        in_specs=[SMEM] + [VMEM] * 3,
        out_specs=[VMEM] * parts,
        name="split_qkv",
    )(me, query[0], key[0], value[0])
    pieces = exchange(sent, 1)

    cot_late, _ = lax.optimization_barrier((cot, sent[0]))
    place, packed_grads = pl.pallas_call(
        functools.partial(place_kernel, owners),
        out_shape=[sds((TOP, 3, owners * 8, tokens), BF), wire],
        in_specs=[VMEM] * 3,
        out_specs=[VMEM] * 2,
        name="place",
    )(route, gate, cot_late)
    grad_wire = swap(packed_grads)

    attended_pieces = pl.pallas_call(
        functools.partial(attend_kernel, parts),
        out_shape=[single] * parts + [sds((heads, length, length), BF)],
        in_specs=[VMEM] * parts,
        out_specs=[VMEM] * (parts + 1),
        scratch_shapes=[pltpu.VMEM((length, width), BF)] * 2,
        compiler_params=BIG,
        cost_estimate=HEAVY,
        name="attend",
    )(*pieces)
    probs = attended_pieces[parts]
    attended_pieces = exchange(attended_pieces[:parts], -1)

    attended, packed = pl.pallas_call(
        functools.partial(norm_kernel, parts),
        out_shape=[sds((tokens, model), BF), wire],
        in_specs=[SMEM] + [VMEM] * (parts + 1),
        out_specs=[VMEM] * 2,
        name="norm_pack",
    )(me, place, *attended_pieces)
    wire_rows = swap(packed)

    blocks = 4
    chunk = hidden // blocks
    whole_wire = pl.BlockSpec(wire.shape, lambda i: (0, 0, 0))
    dact, turned = pl.pallas_call(
        functools.partial(dact_kernel, pairs, parts),
        grid=(blocks,),
        out_shape=[sds((slots, hidden), F32), sds((model, slots), BF)],
        in_specs=[VMEM, pl.BlockSpec((chunk, model), lambda i: (i, 0))],
        out_specs=[
            pl.BlockSpec((slots, chunk), lambda i: (0, i)),
            pl.BlockSpec((model, slots), lambda i: (0, 0)),
        ],
        scratch_shapes=[pltpu.VMEM((slots, model), BF)],
        compiler_params=BIG,
        name="dact",
    )(grad_wire, down)
    both, rows, dnormed = pl.pallas_call(
        expert_kernel,
        grid=(blocks,),
        out_shape=[sds((2, slots, hidden), BF), sds((slots, model), BF), wire],
        in_specs=[
            VMEM,
            pl.BlockSpec((model, chunk), lambda i: (0, i)),
            pl.BlockSpec((slots, chunk), lambda i: (0, i)),
        ],
        out_specs=[
            pl.BlockSpec((2, slots, chunk), lambda i: (0, 0, i)),
            pl.BlockSpec((slots, model), lambda i: (0, 0)),
            whole_wire,
        ],
        scratch_shapes=[pltpu.VMEM((slots, model), F32)],
        compiler_params=BIG,
        name="expert",
    )(wire_rows, up, dact)
    dnormed_back = swap(dnormed)

    half = hidden // 2
    partial_grads = pl.pallas_call(
        functools.partial(weight_grad_kernel, pairs, parts, 2),
        grid=(4,),
        out_shape=sds((model, 2 * hidden), BF),
        in_specs=[
            pl.BlockSpec((1, slots, half), lambda i: (lax.div(i, 2), 0, lax.rem(i, 2))),
            pl.BlockSpec((model, slots), lambda i: (0, 0)),
            pl.BlockSpec((slots, model), lambda i: (0, 0)),
        ],
        out_specs=pl.BlockSpec((model, half), lambda i: (0, i)),
        scratch_shapes=[pltpu.VMEM((model, slots), BF)],
        compiler_params=BIG,
        name="weight_grads",
    )(both, turned, rows)
    sums = lax.psum_scatter(partial_grads, ("seq", "dp"), scatter_dimension=0, tiled=True)

    both_late, _ = lax.optimization_barrier((both, partial_grads))
    produced = pl.pallas_call(
        out_kernel,
        grid=(blocks,),
        out_shape=wire,
        in_specs=[
            pl.BlockSpec((1, slots, chunk), lambda i: (0, 0, i)),
            pl.BlockSpec((chunk, model), lambda i: (i, 0)),
        ],
        out_specs=whole_wire,
        scratch_shapes=[pltpu.VMEM((slots, model), F32)],
        compiler_params=BIG,
        cost_estimate=HEAVY,
        name="expert_out",
    )(both_late, down)

    dnormed_back, produced = lax.optimization_barrier((dnormed_back, produced))
    grad_pieces = pl.pallas_call(
        functools.partial(dattended_kernel, parts),
        out_shape=[single] * parts,
        in_specs=[SMEM] + [VMEM] * 4,
        out_specs=[VMEM] * parts,
        scratch_shapes=[pltpu.VMEM((tokens, model), BF)],
        name="dattended",
    )(me, place, dnormed_back, attended, cot)
    grad_pieces = exchange(grad_pieces, 1)

    produced_back = swap(produced)

    back_pieces = pl.pallas_call(
        functools.partial(attend_back_kernel, parts),
        out_shape=[triple] * parts,
        in_specs=[VMEM] * (2 * parts + 1),
        out_specs=[VMEM] * parts,
        scratch_shapes=[pltpu.VMEM((length, width), BF)] * 2
        + [pltpu.VMEM((length, width), F32)] * 2,
        compiler_params=BIG,
        cost_estimate=MIDDLE,
        name="attend_back",
    )(*pieces, *grad_pieces, probs)
    back_pieces = exchange(back_pieces, -1)

    band = model // (pairs * parts)
    layer_output, grad_queries, grad_keys, grad_values, grad_up, grad_down = pl.pallas_call(
        functools.partial(finish_kernel, parts),
        out_shape=[sds((tokens, model), BF)] * 4 + [sds((band, hidden), F32), sds((hidden, band), F32)],
        in_specs=[SMEM] + [VMEM] * (parts + 5),
        out_specs=[VMEM] * 6,
        compiler_params=BIG,
        name="finish",
    )(me, sums, place, produced_back, attended, gate, *back_pieces)
    return (
        layer_output[None],
        grad_queries[None],
        grad_keys[None],
        grad_values[None],
        grad_up[None],
        grad_down[None],
    )


def solution(mesh):
    rows = P(("dp", "expert"), "seq", None)
    weight = P("expert", None, None)
    return jax.shard_map(
        shards,
        mesh=mesh,
        in_specs=(rows, rows, rows, rows, rows, weight, weight, rows),
        out_specs=(rows, rows, rows, rows, P("expert", ("dp", "seq"), None), P("expert", None, ("dp", "seq"))),
        check_vma=False,
    )
```

```python
import functools
import math

import jax
import jax.numpy as jnp
from jax import lax
from jax.experimental import pallas as pl
from jax.experimental.pallas import tpu as pltpu
from jax.sharding import PartitionSpec as P

DH = 128
TOP = 2
EPSILON = 1e-06
GELU_COEF = math.sqrt(2.0 / math.pi)
BF = jnp.bfloat16
F32 = jnp.float32
VMEM = pl.BlockSpec(memory_space=pltpu.VMEM)
SMEM = pl.BlockSpec(memory_space=pltpu.SMEM)
NN = (((1,), (0,)), ((), ()))
NT = (((1,), (1,)), ((), ()))
TN = (((0,), (0,)), ((), ()))
HEAVY = pl.CostEstimate(flops=1_000_000_000_000, transcendentals=0, bytes_accessed=1_000_000)
MIDDLE = pl.CostEstimate(flops=40_000_000_000, transcendentals=0, bytes_accessed=1_000_000)
BIG = pltpu.CompilerParams(vmem_limit_bytes=56 * 1024 * 1024)


def dot(a, b, dims=NN):
    return lax.dot_general(a, b, dims, preferred_element_type=F32)


def sds(shape, dtype):
    return jax.ShapeDtypeStruct(shape, dtype)


def near(array):
    return pltpu.with_memory_space_constraint(array, pltpu.VMEM)


def lane_block(me, step, parts, width):
    return pl.ds(pl.multiple_of(lax.rem(me + step, parts) * width, width), width)


def split_kernel(parts, me_ref, q_ref, k_ref, v_ref, *outs):
    me = me_ref[0]
    rows = q_ref.shape[0]
    width = q_ref.shape[1] // parts
    for step in range(parts):
        lanes = lane_block(me, step, parts, width)
        for i, ref in enumerate((q_ref, k_ref, v_ref)):
            outs[step][i * rows:(i + 1) * rows, :] = ref[:, lanes]


def join_kernel(parts, me_ref, *refs):
    me = me_ref[0]
    pieces, outs = refs[:parts], refs[parts:]
    rows = outs[0].shape[0]
    width = outs[0].shape[1] // parts
    for step in range(parts):
        lanes = lane_block(me, step, parts, width)
        for i, ref in enumerate(outs):
            ref[:, lanes] = pieces[step][i * rows:(i + 1) * rows, :]


def attend_kernel(parts, *refs):
    pieces = refs[:parts]
    outs = refs[parts:2 * parts]
    probs_ref, keys, values = refs[2 * parts:]
    rows = outs[0].shape[0]
    width = outs[0].shape[1]
    scaling = 1.0 / math.sqrt(DH)
    for step in range(parts):
        keys[step * rows:(step + 1) * rows, :] = pieces[step][rows:2 * rows, :]
        values[step * rows:(step + 1) * rows, :] = pieces[step][2 * rows:3 * rows, :]
    for head in range(width // DH):
        lanes = slice(head * DH, (head + 1) * DH)
        for step in range(parts):
            scores = dot(pieces[step][0:rows, lanes], keys[:, lanes], NT) * scaling
            exponent = jnp.exp(scores - jnp.max(scores, axis=-1, keepdims=True))
            probs = exponent / jnp.sum(exponent, axis=-1, keepdims=True)
            rounded = probs.astype(BF)
            probs_ref[head, step * rows:(step + 1) * rows, :] = rounded
            outs[step][:, lanes] = dot(rounded, values[:, lanes]).astype(BF)


def attend_back_kernel(parts, *refs):
    pieces = refs[:parts]
    grads = refs[parts:2 * parts]
    probs_ref = refs[2 * parts]
    outs = refs[2 * parts + 1:3 * parts + 1]
    keys, values, grad_keys, grad_values = refs[3 * parts + 1:]
    rows = grads[0].shape[0]
    width = grads[0].shape[1]
    scaling = 1.0 / math.sqrt(DH)
    for step in range(parts):
        keys[step * rows:(step + 1) * rows, :] = pieces[step][rows:2 * rows, :]
        values[step * rows:(step + 1) * rows, :] = pieces[step][2 * rows:3 * rows, :]
    for head in range(width // DH):
        lanes = slice(head * DH, (head + 1) * DH)
        for step in range(parts):
            query = pieces[step][0:rows, lanes]
            grad = grads[step][:, lanes]
            rounded = probs_ref[head, step * rows:(step + 1) * rows, :]
            probs = rounded.astype(F32)
            grad_probs = dot(grad, values[:, lanes], NT)
            delta = jnp.sum(probs * grad_probs, axis=-1, keepdims=True)
            grad_scores = (probs * (grad_probs - delta) * scaling).astype(BF)
            outs[step][0:rows, lanes] = dot(grad_scores, keys[:, lanes]).astype(BF)
            key_part = dot(grad_scores, query, TN)
            value_part = dot(rounded, grad, TN)
            if step == 0:
                grad_keys[:, lanes] = key_part
                grad_values[:, lanes] = value_part
            else:
                grad_keys[:, lanes] += key_part
                grad_values[:, lanes] += value_part
    for step in range(parts):
        outs[step][rows:2 * rows, :] = grad_keys[step * rows:(step + 1) * rows, :].astype(BF)
        outs[step][2 * rows:3 * rows, :] = grad_values[step * rows:(step + 1) * rows, :].astype(BF)


def chunk_of(array, c):
    return array[:, c * 128:(c + 1) * 128]


def lane_cat(pieces):
    return jnp.concatenate(pieces, axis=1)


def half_pickers(owners):
    shape = (owners * 4, owners * 8)
    row = lax.broadcasted_iota(jnp.int32, shape, 0)
    col = lax.broadcasted_iota(jnp.int32, shape, 1)
    first = lax.shift_left(lax.shift_right_logical(row, 2), 3) + lax.bitwise_and(row, 3)
    return [(col == first + 4 * half).astype(F32).astype(BF) for half in range(2)]


def read_tiles(ref):
    owners, lines, _ = ref.shape
    tiles = [
        ref[:, 8 * t:8 * t + 8, :].astype(F32).reshape(owners * 8, 128).astype(BF)
        for t in range(lines // 8)
    ]
    count = len(tiles) * 2 // 3
    return tiles[:count], lane_cat(tiles[count:])


def write_tiles(ref, low, high):
    owners = ref.shape[0]
    count = low.shape[1] // 128
    for c in range(count):
        ref[:, 8 * c:8 * c + 8, :] = chunk_of(low, c).reshape(owners, 8, 128).astype(BF)
    for c in range(count // 2):
        start = 8 * (count + c)
        ref[:, start:start + 8, :] = chunk_of(high, c).reshape(owners, 8, 128).astype(BF)


def split_parity(array):
    count = array.shape[1] // 128
    return [lane_cat([chunk_of(array, c) for c in range(half, count, 2)]) for half in range(2)]


def merge_parity(even, odd):
    count = even.shape[1] // 128
    return lane_cat([chunk_of(part, c) for c in range(count) for part in (even, odd)])


def unpack_rows(ref, out_ref):
    low, high = read_tiles(ref)
    owners = ref.shape[0]
    even, odd = [dot(pick, high).astype(BF) for pick in half_pickers(owners)]
    out_ref[0:owners * 8, :] = lane_cat(low)
    out_ref[owners * 8:, :] = merge_parity(even, odd)


def pack_rows(rows, ref):
    owners = ref.shape[0]
    pickers = half_pickers(owners)
    parts = split_parity(rows[owners * 8:, :].astype(BF))
    high = dot(pickers[0], parts[0], TN) + dot(pickers[1], parts[1], TN)
    write_tiles(ref, rows[0:owners * 8, :], high)


def pack_tokens(places, arrays, ref):
    low = sum([dot(place[0], x) for place, x in zip(places, arrays)])
    high = None
    for place, x in zip(places, arrays):
        for half, part in enumerate(split_parity(x)):
            term = dot(place[1 + half], part)
            high = term if high is None else high + term
    write_tiles(ref, low, high)


def unpack_tokens(place, low, high):
    even, odd = [dot(place[1 + half], high, TN) for half in range(2)]
    return dot(place[0], lane_cat(low), TN) + merge_parity(even, odd)


def column(row):
    side = row.shape[1]
    return jnp.broadcast_to(row, (side, side)).T[:, 0:1]


def place_kernel(experts, routes_ref, gates_ref, cot_ref, place_ref, packed_ref):
    tokens = cot_ref.shape[0]
    first = lax.broadcasted_iota(jnp.int32, (tokens, tokens), 0)
    second = lax.broadcasted_iota(jnp.int32, (tokens, tokens), 1)
    earlier = (first < second).astype(F32).astype(BF)
    expert_ids = lax.broadcasted_iota(jnp.int32, (experts, tokens), 0)
    line_ids = lax.broadcasted_iota(jnp.int32, (experts * 8, tokens), 0)
    routes = [routes_ref[j:j + 1, :] for j in range(TOP)]
    hits = [(route == expert_ids).astype(F32) for route in routes]
    before = dot(sum(hits[1:], hits[0]).astype(BF), earlier)
    upstream = cot_ref[...].astype(F32)
    places, arrays = [], []
    for j in range(TOP):
        rank = jnp.sum(before * hits[j], axis=0, keepdims=True).astype(jnp.int32)
        line = routes[j] * 8 + rank
        targets = (
            jnp.where(rank < 8, line, -1),
            jnp.where(rank >= 8, line - 8, -1),
            jnp.where(rank >= 8, line - 4, -1),
        )
        place = [(line_ids == target).astype(F32).astype(BF) for target in targets]
        for i, part in enumerate(place):
            place_ref[j, i] = part
        places.append(place)
        arrays.append((column(gates_ref[j:j + 1, :]) * upstream).astype(BF))
    pack_tokens(places, arrays, packed_ref)


def inverse_rms_of(attended):
    return lax.rsqrt(jnp.mean(attended * attended, axis=-1, keepdims=True) + EPSILON)


def joint_place(place_ref):
    joint = []
    for i in range(3):
        part = place_ref[0, i]
        for j in range(1, TOP):
            part = part + place_ref[j, i]
        joint.append(part)
    return joint


def norm_kernel(parts, me_ref, place_ref, *refs):
    pieces, (attended_ref, packed_ref) = refs[:parts], refs[parts:]
    me = me_ref[0]
    width = pieces[0].shape[1]
    for step in range(parts):
        attended_ref[:, lane_block(me, step, parts, width)] = pieces[step][...]
    attended = attended_ref[...].astype(F32)
    normed = (attended * inverse_rms_of(attended)).astype(BF)
    pack_tokens([joint_place(place_ref)], [normed], packed_ref)


def turn_rows(pairs, parts, rows_ref, turned_ref):
    band = rows_ref.shape[1] // (pairs * parts)
    for s in range(pairs * parts):
        block = (s % pairs) * parts + s // pairs
        turned_ref[s * band:(s + 1) * band, :] = rows_ref[:, block * band:(block + 1) * band].T


def dact_kernel(pairs, parts, packed_ref, down_ref, out_ref, turned_ref, rows):
    @pl.when(pl.program_id(0) == 0)
    def _():
        unpack_rows(packed_ref, rows)
        turn_rows(pairs, parts, rows, turned_ref)

    out_ref[...] = dot(rows[...], down_ref[...], NT)


def expert_kernel(pairs, parts, packed_ref, up_ref, dact_ref, grads_turned_ref, act_ref, grads_ref, dnormed_ref, rows, turned, total):
    step = pl.program_id(0)

    @pl.when(step == 0)
    def _():
        unpack_rows(packed_ref, rows)
        turn_rows(pairs, parts, rows, turned)

    chunk = up_ref.shape[1]
    pre = dot(rows[...], up_ref[...])
    square = pre * pre
    half = 0.5 + 0.5 * jnp.tanh(pre * (GELU_COEF + (GELU_COEF * 0.044715) * square))
    act = pre * half
    act_rounded = act.astype(BF)
    act_ref[...] = act_rounded
    slope = half + act * (1.0 - half) * (2.0 * GELU_COEF + (6.0 * GELU_COEF * 0.044715) * square)
    dpre = (dact_ref[...] * slope).astype(BF)
    grads_ref[:, 0:chunk] = dot(grads_turned_ref[...], act_rounded).astype(BF)
    grads_ref[:, chunk:] = dot(turned[...], dpre).astype(BF)
    part = dot(dpre, up_ref[...], NT)

    @pl.when(step == 0)
    def _():
        total[...] = part

    @pl.when(step > 0)
    def _():
        total[...] += part

    @pl.when(step == pl.num_programs(0) - 1)
    def _():
        pack_rows(total[...], dnormed_ref)


def out_kernel(hidden_ref, weight_ref, packed_ref, total):
    step = pl.program_id(0)
    part = dot(hidden_ref[...], weight_ref[...])

    @pl.when(step == 0)
    def _():
        total[...] = part

    @pl.when(step > 0)
    def _():
        total[...] += part

    @pl.when(step == pl.num_programs(0) - 1)
    def _():
        pack_rows(total[...], packed_ref)


def dattended_kernel(parts, me_ref, place_ref, back_ref, attended_ref, cot_ref, *refs):
    outs, full = refs[:parts], refs[parts]
    me = me_ref[0]
    low, high = read_tiles(back_ref)
    grad_unit = unpack_tokens(joint_place(place_ref), low, high)
    attended = attended_ref[...].astype(F32)
    inverse_rms = inverse_rms_of(attended)
    unit = attended * inverse_rms
    grad = cot_ref[...].astype(F32) + inverse_rms * (
        grad_unit - unit * jnp.mean(grad_unit * unit, axis=-1, keepdims=True)
    )
    full[...] = grad.astype(BF)
    width = outs[0].shape[1]
    for step in range(parts):
        outs[step][...] = full[:, lane_block(me, step, parts, width)]


def mix_kernel(place_ref, back_ref, attended_ref, gates_ref, out_ref):
    low, high = read_tiles(back_ref)
    mix = None
    for j in range(TOP):
        place = [place_ref[j, i] for i in range(3)]
        term = column(gates_ref[j:j + 1, :]) * unpack_tokens(place, low, high)
        mix = term if mix is None else mix + term
    out_ref[...] = (attended_ref[...].astype(F32) + mix).astype(BF)


def widen_kernel(blocks, sums_ref, up_out, down_out):
    chunk = up_out.shape[1] // blocks
    for i in range(blocks):
        start = 2 * i * chunk
        rows = slice(i * chunk, (i + 1) * chunk)
        down_out[rows, :] = sums_ref[:, start:start + chunk].astype(F32).T
        up_out[:, rows] = sums_ref[:, start + chunk:start + 2 * chunk].astype(F32)


def finish_kernel(parts, blocks, me_ref, sums_ref, place_ref, back_ref, attended_ref, gates_ref, *refs):
    pieces, outs = refs[:parts], refs[parts:]
    widen_kernel(blocks, sums_ref, *outs[4:])
    mix_kernel(place_ref, back_ref, attended_ref, gates_ref, outs[0])
    join_kernel(parts, me_ref, *pieces, *outs[1:4])


def shards(query, key, value, routes, gates, up, down, cotangent):
    tokens, model = query.shape[1:]
    owners = lax.axis_size("expert")
    parts = lax.axis_size("seq")
    pairs = lax.axis_size("dp")
    capacity = tokens * TOP * 3 // (2 * owners)
    slots = owners * capacity
    hidden = up.shape[2]
    width = model // parts
    length = tokens * parts
    heads = width // DH
    up, down = up[0], down[0]
    cot = cotangent[0]
    route, gate = routes[0].T, gates[0].T
    me = jnp.reshape(lax.axis_index("seq"), (1,)).astype(jnp.int32)

    def shift(piece, step):
        pairs_of = [(i, (i + step) % parts) for i in range(parts)]
        return near(lax.ppermute(piece, "seq", pairs_of))

    def swap(packed):
        return near(lax.all_to_all(packed, "expert", split_axis=0, concat_axis=0, tiled=True))

    order = (2, 1, 3) if parts == 4 else tuple(range(1, parts))

    def exchange(pieces, sign):
        moved = {step: shift(pieces[step], sign * step) for step in order}
        return [pieces[0]] + [moved[step] for step in range(1, parts)]

    triple = sds((3 * tokens, width), BF)
    single = sds((tokens, width), BF)
    wire = sds((owners, capacity * model // 128, 128), BF)
    sent = pl.pallas_call(
        functools.partial(split_kernel, parts),
        out_shape=[triple] * parts,
        in_specs=[SMEM] + [VMEM] * 3,
        out_specs=[VMEM] * parts,
        name="split_qkv",
    )(me, query[0], key[0], value[0])
    pieces = exchange(sent, 1)

    cot_late, _ = lax.optimization_barrier((cot, sent[0]))
    place, packed_grads = pl.pallas_call(
        functools.partial(place_kernel, owners),
        out_shape=[sds((TOP, 3, owners * 8, tokens), BF), wire],
        in_specs=[VMEM] * 3,
        out_specs=[VMEM] * 2,
        name="place",
    )(route, gate, cot_late)
    grad_wire = swap(packed_grads)

    attended_pieces = pl.pallas_call(
        functools.partial(attend_kernel, parts),
        out_shape=[single] * parts + [sds((heads, length, length), BF)],
        in_specs=[VMEM] * parts,
        out_specs=[VMEM] * (parts + 1),
        scratch_shapes=[pltpu.VMEM((length, width), BF)] * 2,
        compiler_params=BIG,
        cost_estimate=HEAVY,
        name="attend",
    )(*pieces)
    probs = attended_pieces[parts]
    attended_pieces = exchange(attended_pieces[:parts], -1)

    attended, packed = pl.pallas_call(
        functools.partial(norm_kernel, parts),
        out_shape=[sds((tokens, model), BF), wire],
        in_specs=[SMEM] + [VMEM] * (parts + 1),
        out_specs=[VMEM] * 2,
        name="norm_pack",
    )(me, place, *attended_pieces)
    wire_rows = swap(packed)

    blocks = 4
    chunk = hidden // blocks
    whole_wire = pl.BlockSpec(wire.shape, lambda i: (0, 0, 0))
    dact, turned = pl.pallas_call(
        functools.partial(dact_kernel, pairs, parts),
        grid=(blocks,),
        out_shape=[sds((slots, hidden), F32), sds((model, slots), BF)],
        in_specs=[VMEM, pl.BlockSpec((chunk, model), lambda i: (i, 0))],
        out_specs=[
            pl.BlockSpec((slots, chunk), lambda i: (0, i)),
            pl.BlockSpec((model, slots), lambda i: (0, 0)),
        ],
        scratch_shapes=[pltpu.VMEM((slots, model), BF)],
        compiler_params=BIG,
        name="dact",
    )(grad_wire, down)
    act, partial_grads, dnormed = pl.pallas_call(
        functools.partial(expert_kernel, pairs, parts),
        grid=(blocks,),
        out_shape=[sds((slots, hidden), BF), sds((model, 2 * hidden), BF), wire],
        in_specs=[
            VMEM,
            pl.BlockSpec((model, chunk), lambda i: (0, i)),
            pl.BlockSpec((slots, chunk), lambda i: (0, i)),
            pl.BlockSpec((model, slots), lambda i: (0, 0)),
        ],
        out_specs=[
            pl.BlockSpec((slots, chunk), lambda i: (0, i)),
            pl.BlockSpec((model, 2 * chunk), lambda i: (0, i)),
            whole_wire,
        ],
        scratch_shapes=[
            pltpu.VMEM((slots, model), BF),
            pltpu.VMEM((model, slots), BF),
            pltpu.VMEM((slots, model), F32),
        ],
        compiler_params=BIG,
        name="expert",
    )(wire_rows, up, dact, turned)
    sums = lax.psum_scatter(partial_grads, ("seq", "dp"), scatter_dimension=0, tiled=True)
    dnormed_back = swap(dnormed)
    act_late, _ = lax.optimization_barrier((act, partial_grads))
    produced = pl.pallas_call(
        out_kernel,
        grid=(blocks,),
        out_shape=wire,
        in_specs=[
            pl.BlockSpec((slots, chunk), lambda i: (0, i)),
            pl.BlockSpec((chunk, model), lambda i: (i, 0)),
        ],
        out_specs=whole_wire,
        scratch_shapes=[pltpu.VMEM((slots, model), F32)],
        compiler_params=BIG,
        cost_estimate=HEAVY,
        name="expert_out",
    )(act_late, down)

    dnormed_back, produced = lax.optimization_barrier((dnormed_back, produced))
    grad_pieces = pl.pallas_call(
        functools.partial(dattended_kernel, parts),
        out_shape=[single] * parts,
        in_specs=[SMEM] + [VMEM] * 4,
        out_specs=[VMEM] * parts,
        scratch_shapes=[pltpu.VMEM((tokens, model), BF)],
        name="dattended",
    )(me, place, dnormed_back, attended, cot)
    grad_pieces = exchange(grad_pieces, 1)

    produced_back = swap(produced)

    back_pieces = pl.pallas_call(
        functools.partial(attend_back_kernel, parts),
        out_shape=[triple] * parts,
        in_specs=[VMEM] * (2 * parts + 1),
        out_specs=[VMEM] * parts,
        scratch_shapes=[pltpu.VMEM((length, width), BF)] * 2
        + [pltpu.VMEM((length, width), F32)] * 2,
        compiler_params=BIG,
        cost_estimate=MIDDLE,
        name="attend_back",
    )(*pieces, *grad_pieces, probs)
    back_pieces = exchange(back_pieces, -1)

    band = model // (pairs * parts)
    layer_output, grad_queries, grad_keys, grad_values, grad_up, grad_down = pl.pallas_call(
        functools.partial(finish_kernel, parts, blocks),
        out_shape=[sds((tokens, model), BF)] * 4 + [sds((band, hidden), F32), sds((hidden, band), F32)],
        in_specs=[SMEM] + [VMEM] * (parts + 5),
        out_specs=[VMEM] * 6,
        compiler_params=BIG,
        name="finish",
    )(me, sums, place, produced_back, attended, gate, *back_pieces)
    return (
        layer_output[None],
        grad_queries[None],
        grad_keys[None],
        grad_values[None],
        grad_up[None],
        grad_down[None],
    )


def solution(mesh):
    rows = P(("dp", "expert"), "seq", None)
    weight = P("expert", None, None)
    return jax.shard_map(
        shards,
        mesh=mesh,
        in_specs=(rows, rows, rows, rows, rows, weight, weight, rows),
        out_specs=(rows, rows, rows, rows, P("expert", ("dp", "seq"), None), P("expert", None, ("dp", "seq"))),
        check_vma=False,
    )
```

```python
import functools
import math

import jax
import jax.numpy as jnp
from jax import lax
from jax.experimental import pallas as pl
from jax.experimental.pallas import tpu as pltpu
from jax.sharding import PartitionSpec as P

DH = 128
TOP = 2
EPSILON = 1e-06
GELU_COEF = math.sqrt(2.0 / math.pi)
BF = jnp.bfloat16
F32 = jnp.float32
VMEM = pl.BlockSpec(memory_space=pltpu.VMEM)
SMEM = pl.BlockSpec(memory_space=pltpu.SMEM)
NN = (((1,), (0,)), ((), ()))
NT = (((1,), (1,)), ((), ()))
TN = (((0,), (0,)), ((), ()))
HEAVY = pl.CostEstimate(flops=1_000_000_000_000, transcendentals=0, bytes_accessed=1_000_000)
MIDDLE = pl.CostEstimate(flops=40_000_000_000, transcendentals=0, bytes_accessed=1_000_000)
BIG = pltpu.CompilerParams(vmem_limit_bytes=56 * 1024 * 1024)


def dot(a, b, dims=NN):
    return lax.dot_general(a, b, dims, preferred_element_type=F32)


def sds(shape, dtype):
    return jax.ShapeDtypeStruct(shape, dtype)


def near(array):
    return pltpu.with_memory_space_constraint(array, pltpu.VMEM)


def lane_block(me, step, parts, width):
    return pl.ds(pl.multiple_of(lax.rem(me + step, parts) * width, width), width)


def split_kernel(parts, me_ref, q_ref, k_ref, v_ref, *outs):
    me = me_ref[0]
    rows = q_ref.shape[0]
    width = q_ref.shape[1] // parts
    for step in range(parts):
        lanes = lane_block(me, step, parts, width)
        for i, ref in enumerate((q_ref, k_ref, v_ref)):
            outs[step][i * rows:(i + 1) * rows, :] = ref[:, lanes]


def join_kernel(parts, me_ref, *refs):
    me = me_ref[0]
    pieces, outs = refs[:parts], refs[parts:]
    rows = outs[0].shape[0]
    width = outs[0].shape[1] // parts
    for step in range(parts):
        lanes = lane_block(me, step, parts, width)
        for i, ref in enumerate(outs):
            ref[:, lanes] = pieces[step][i * rows:(i + 1) * rows, :]


def attend_kernel(parts, *refs):
    pieces = refs[:parts]
    outs = refs[parts:2 * parts]
    probs_ref, keys, values = refs[2 * parts:]
    rows = outs[0].shape[0]
    width = outs[0].shape[1]
    scaling = 1.0 / math.sqrt(DH)
    for step in range(parts):
        keys[step * rows:(step + 1) * rows, :] = pieces[step][rows:2 * rows, :]
        values[step * rows:(step + 1) * rows, :] = pieces[step][2 * rows:3 * rows, :]
    for head in range(width // DH):
        lanes = slice(head * DH, (head + 1) * DH)
        for step in range(parts):
            scores = dot(pieces[step][0:rows, lanes], keys[:, lanes], NT) * scaling
            exponent = jnp.exp(scores - jnp.max(scores, axis=-1, keepdims=True))
            probs = exponent / jnp.sum(exponent, axis=-1, keepdims=True)
            rounded = probs.astype(BF)
            probs_ref[head, step * rows:(step + 1) * rows, :] = rounded
            outs[step][:, lanes] = dot(rounded, values[:, lanes]).astype(BF)


def attend_back_kernel(parts, *refs):
    pieces = refs[:parts]
    grads = refs[parts:2 * parts]
    probs_ref = refs[2 * parts]
    outs = refs[2 * parts + 1:3 * parts + 1]
    keys, values, grad_keys, grad_values = refs[3 * parts + 1:]
    rows = grads[0].shape[0]
    width = grads[0].shape[1]
    scaling = 1.0 / math.sqrt(DH)
    for step in range(parts):
        keys[step * rows:(step + 1) * rows, :] = pieces[step][rows:2 * rows, :]
        values[step * rows:(step + 1) * rows, :] = pieces[step][2 * rows:3 * rows, :]
    for head in range(width // DH):
        lanes = slice(head * DH, (head + 1) * DH)
        for step in range(parts):
            query = pieces[step][0:rows, lanes]
            grad = grads[step][:, lanes]
            rounded = probs_ref[head, step * rows:(step + 1) * rows, :]
            probs = rounded.astype(F32)
            grad_probs = dot(grad, values[:, lanes], NT)
            delta = jnp.sum(probs * grad_probs, axis=-1, keepdims=True)
            grad_scores = (probs * (grad_probs - delta) * scaling).astype(BF)
            outs[step][0:rows, lanes] = dot(grad_scores, keys[:, lanes]).astype(BF)
            key_part = dot(grad_scores, query, TN)
            value_part = dot(rounded, grad, TN)
            if step == 0:
                grad_keys[:, lanes] = key_part
                grad_values[:, lanes] = value_part
            else:
                grad_keys[:, lanes] += key_part
                grad_values[:, lanes] += value_part
    for step in range(parts):
        outs[step][rows:2 * rows, :] = grad_keys[step * rows:(step + 1) * rows, :].astype(BF)
        outs[step][2 * rows:3 * rows, :] = grad_values[step * rows:(step + 1) * rows, :].astype(BF)


def chunk_of(array, c):
    return array[:, c * 128:(c + 1) * 128]


def lane_cat(pieces):
    return jnp.concatenate(pieces, axis=1)


def half_pickers(owners):
    shape = (owners * 4, owners * 8)
    row = lax.broadcasted_iota(jnp.int32, shape, 0)
    col = lax.broadcasted_iota(jnp.int32, shape, 1)
    first = lax.shift_left(lax.shift_right_logical(row, 2), 3) + lax.bitwise_and(row, 3)
    return [(col == first + 4 * half).astype(F32).astype(BF) for half in range(2)]


def read_tiles(ref):
    owners, lines, _ = ref.shape
    tiles = [
        ref[:, 8 * t:8 * t + 8, :].astype(F32).reshape(owners * 8, 128).astype(BF)
        for t in range(lines // 8)
    ]
    count = len(tiles) * 2 // 3
    return tiles[:count], lane_cat(tiles[count:])


def write_tiles(ref, low, high):
    owners = ref.shape[0]
    count = low.shape[1] // 128
    for c in range(count):
        ref[:, 8 * c:8 * c + 8, :] = chunk_of(low, c).reshape(owners, 8, 128).astype(BF)
    for c in range(count // 2):
        start = 8 * (count + c)
        ref[:, start:start + 8, :] = chunk_of(high, c).reshape(owners, 8, 128).astype(BF)


def split_parity(array):
    count = array.shape[1] // 128
    return [lane_cat([chunk_of(array, c) for c in range(half, count, 2)]) for half in range(2)]


def merge_parity(even, odd):
    count = even.shape[1] // 128
    return lane_cat([chunk_of(part, c) for c in range(count) for part in (even, odd)])


def unpack_rows(ref, out_ref):
    low, high = read_tiles(ref)
    owners = ref.shape[0]
    even, odd = [dot(pick, high).astype(BF) for pick in half_pickers(owners)]
    out_ref[0:owners * 8, :] = lane_cat(low)
    out_ref[owners * 8:, :] = merge_parity(even, odd)


def pack_rows(rows, ref):
    owners = ref.shape[0]
    pickers = half_pickers(owners)
    parts = split_parity(rows[owners * 8:, :].astype(BF))
    high = dot(pickers[0], parts[0], TN) + dot(pickers[1], parts[1], TN)
    write_tiles(ref, rows[0:owners * 8, :], high)


def pack_tokens(places, arrays, ref):
    low = sum([dot(place[0], x) for place, x in zip(places, arrays)])
    high = None
    for place, x in zip(places, arrays):
        for half, part in enumerate(split_parity(x)):
            term = dot(place[1 + half], part)
            high = term if high is None else high + term
    write_tiles(ref, low, high)


def unpack_tokens(place, low, high):
    even, odd = [dot(place[1 + half], high, TN) for half in range(2)]
    return dot(place[0], lane_cat(low), TN) + merge_parity(even, odd)


def column(row):
    side = row.shape[1]
    return jnp.broadcast_to(row, (side, side)).T[:, 0:1]


def place_kernel(experts, routes_ref, gates_ref, cot_ref, place_ref, packed_ref):
    tokens = cot_ref.shape[0]
    first = lax.broadcasted_iota(jnp.int32, (tokens, tokens), 0)
    second = lax.broadcasted_iota(jnp.int32, (tokens, tokens), 1)
    earlier = (first < second).astype(F32).astype(BF)
    expert_ids = lax.broadcasted_iota(jnp.int32, (experts, tokens), 0)
    line_ids = lax.broadcasted_iota(jnp.int32, (experts * 8, tokens), 0)
    routes = [routes_ref[j:j + 1, :] for j in range(TOP)]
    hits = [(route == expert_ids).astype(F32) for route in routes]
    before = dot(sum(hits[1:], hits[0]).astype(BF), earlier)
    upstream = cot_ref[...].astype(F32)
    places, arrays = [], []
    for j in range(TOP):
        rank = jnp.sum(before * hits[j], axis=0, keepdims=True).astype(jnp.int32)
        line = routes[j] * 8 + rank
        targets = (
            jnp.where(rank < 8, line, -1),
            jnp.where(rank >= 8, line - 8, -1),
            jnp.where(rank >= 8, line - 4, -1),
        )
        place = [(line_ids == target).astype(F32).astype(BF) for target in targets]
        for i, part in enumerate(place):
            place_ref[j, i] = part
        places.append(place)
        arrays.append((column(gates_ref[j:j + 1, :]) * upstream).astype(BF))
    pack_tokens(places, arrays, packed_ref)


def entry_kernel(parts, experts, me_ref, q_ref, k_ref, v_ref, routes_ref, gates_ref, cot_ref, *outs):
    split_kernel(parts, me_ref, q_ref, k_ref, v_ref, *outs[:parts])
    place_kernel(experts, routes_ref, gates_ref, cot_ref, *outs[parts:])


def inverse_rms_of(attended):
    return lax.rsqrt(jnp.mean(attended * attended, axis=-1, keepdims=True) + EPSILON)


def joint_place(place_ref):
    joint = []
    for i in range(3):
        part = place_ref[0, i]
        for j in range(1, TOP):
            part = part + place_ref[j, i]
        joint.append(part)
    return joint


def norm_kernel(parts, me_ref, place_ref, *refs):
    pieces, (attended_ref, packed_ref) = refs[:parts], refs[parts:]
    me = me_ref[0]
    width = pieces[0].shape[1]
    for step in range(parts):
        attended_ref[:, lane_block(me, step, parts, width)] = pieces[step][...]
    attended = attended_ref[...].astype(F32)
    normed = (attended * inverse_rms_of(attended)).astype(BF)
    pack_tokens([joint_place(place_ref)], [normed], packed_ref)


def turn_rows(pairs, parts, rows_ref, turned_ref):
    band = rows_ref.shape[1] // (pairs * parts)
    for s in range(pairs * parts):
        block = (s % pairs) * parts + s // pairs
        turned_ref[s * band:(s + 1) * band, :] = rows_ref[:, block * band:(block + 1) * band].T


def dact_kernel(pairs, parts, packed_ref, down_ref, out_ref, turned_ref, rows):
    @pl.when(pl.program_id(0) == 0)
    def _():
        unpack_rows(packed_ref, rows)
        turn_rows(pairs, parts, rows, turned_ref)

    out_ref[...] = dot(rows[...], down_ref[...], NT)


def expert_kernel(pairs, parts, packed_ref, up_ref, dact_ref, grads_turned_ref, act_ref, grads_ref, dnormed_ref, rows, turned, total):
    step = pl.program_id(0)

    @pl.when(step == 0)
    def _():
        unpack_rows(packed_ref, rows)
        turn_rows(pairs, parts, rows, turned)

    chunk = up_ref.shape[1]
    pre = dot(rows[...], up_ref[...])
    square = pre * pre
    half = 0.5 + 0.5 * jnp.tanh(pre * (GELU_COEF + (GELU_COEF * 0.044715) * square))
    act = pre * half
    act_rounded = act.astype(BF)
    act_ref[...] = act_rounded
    slope = half + act * (1.0 - half) * (2.0 * GELU_COEF + (6.0 * GELU_COEF * 0.044715) * square)
    dpre = (dact_ref[...] * slope).astype(BF)
    grads_ref[:, 0:chunk] = dot(grads_turned_ref[...], act_rounded).astype(BF)
    grads_ref[:, chunk:] = dot(turned[...], dpre).astype(BF)
    part = dot(dpre, up_ref[...], NT)

    @pl.when(step == 0)
    def _():
        total[...] = part

    @pl.when(step > 0)
    def _():
        total[...] += part

    @pl.when(step == pl.num_programs(0) - 1)
    def _():
        pack_rows(total[...], dnormed_ref)


def out_kernel(hidden_ref, weight_ref, packed_ref, total):
    step = pl.program_id(0)
    part = dot(hidden_ref[...], weight_ref[...])

    @pl.when(step == 0)
    def _():
        total[...] = part

    @pl.when(step > 0)
    def _():
        total[...] += part

    @pl.when(step == pl.num_programs(0) - 1)
    def _():
        pack_rows(total[...], packed_ref)


def dattended_kernel(parts, me_ref, place_ref, back_ref, attended_ref, cot_ref, *refs):
    outs, full = refs[:parts], refs[parts]
    me = me_ref[0]
    low, high = read_tiles(back_ref)
    grad_unit = unpack_tokens(joint_place(place_ref), low, high)
    attended = attended_ref[...].astype(F32)
    inverse_rms = inverse_rms_of(attended)
    unit = attended * inverse_rms
    grad = cot_ref[...].astype(F32) + inverse_rms * (
        grad_unit - unit * jnp.mean(grad_unit * unit, axis=-1, keepdims=True)
    )
    full[...] = grad.astype(BF)
    width = outs[0].shape[1]
    for step in range(parts):
        outs[step][...] = full[:, lane_block(me, step, parts, width)]


def mix_kernel(place_ref, back_ref, attended_ref, gates_ref, out_ref):
    low, high = read_tiles(back_ref)
    mix = None
    for j in range(TOP):
        place = [place_ref[j, i] for i in range(3)]
        term = column(gates_ref[j:j + 1, :]) * unpack_tokens(place, low, high)
        mix = term if mix is None else mix + term
    out_ref[...] = (attended_ref[...].astype(F32) + mix).astype(BF)


def widen_kernel(blocks, sums_ref, up_out, down_out):
    chunk = up_out.shape[1] // blocks
    for i in range(blocks):
        start = 2 * i * chunk
        rows = slice(i * chunk, (i + 1) * chunk)
        down_out[rows, :] = sums_ref[:, start:start + chunk].astype(F32).T
        up_out[:, rows] = sums_ref[:, start + chunk:start + 2 * chunk].astype(F32)


def finish_kernel(parts, blocks, me_ref, sums_ref, place_ref, back_ref, attended_ref, gates_ref, *refs):
    pieces, outs = refs[:parts], refs[parts:]
    widen_kernel(blocks, sums_ref, *outs[4:])
    mix_kernel(place_ref, back_ref, attended_ref, gates_ref, outs[0])
    join_kernel(parts, me_ref, *pieces, *outs[1:4])


def shards(query, key, value, routes, gates, up, down, cotangent):
    tokens, model = query.shape[1:]
    owners = lax.axis_size("expert")
    parts = lax.axis_size("seq")
    pairs = lax.axis_size("dp")
    capacity = tokens * TOP * 3 // (2 * owners)
    slots = owners * capacity
    hidden = up.shape[2]
    width = model // parts
    length = tokens * parts
    heads = width // DH
    up, down = up[0], down[0]
    cot = cotangent[0]
    route, gate = routes[0].T, gates[0].T
    me = jnp.reshape(lax.axis_index("seq"), (1,)).astype(jnp.int32)

    def shift(piece, step):
        pairs_of = [(i, (i + step) % parts) for i in range(parts)]
        return near(lax.ppermute(piece, "seq", pairs_of))

    def swap(packed):
        return near(lax.all_to_all(packed, "expert", split_axis=0, concat_axis=0, tiled=True))

    order = (2, 1, 3) if parts == 4 else tuple(range(1, parts))

    def exchange(pieces, sign):
        moved = {step: shift(pieces[step], sign * step) for step in order}
        return [pieces[0]] + [moved[step] for step in range(1, parts)]

    triple = sds((3 * tokens, width), BF)
    single = sds((tokens, width), BF)
    wire = sds((owners, capacity * model // 128, 128), BF)
    *sent, place, packed_grads = pl.pallas_call(
        functools.partial(entry_kernel, parts, owners),
        out_shape=[triple] * parts + [sds((TOP, 3, owners * 8, tokens), BF), wire],
        in_specs=[SMEM] + [VMEM] * 6,
        out_specs=[VMEM] * (parts + 2),
        name="entry",
    )(me, query[0], key[0], value[0], route, gate, cot)
    pieces = exchange(sent, 1)
    grad_wire = swap(packed_grads)

    attended_pieces = pl.pallas_call(
        functools.partial(attend_kernel, parts),
        out_shape=[single] * parts + [sds((heads, length, length), BF)],
        in_specs=[VMEM] * parts,
        out_specs=[VMEM] * (parts + 1),
        scratch_shapes=[pltpu.VMEM((length, width), BF)] * 2,
        compiler_params=BIG,
        cost_estimate=HEAVY,
        name="attend",
    )(*pieces)
    probs = attended_pieces[parts]
    attended_pieces = exchange(attended_pieces[:parts], -1)

    attended, packed = pl.pallas_call(
        functools.partial(norm_kernel, parts),
        out_shape=[sds((tokens, model), BF), wire],
        in_specs=[SMEM] + [VMEM] * (parts + 1),
        out_specs=[VMEM] * 2,
        name="norm_pack",
    )(me, place, *attended_pieces)
    wire_rows = swap(packed)

    blocks = 4
    chunk = hidden // blocks
    whole_wire = pl.BlockSpec(wire.shape, lambda i: (0, 0, 0))
    dact, turned = pl.pallas_call(
        functools.partial(dact_kernel, pairs, parts),
        grid=(blocks,),
        out_shape=[sds((slots, hidden), F32), sds((model, slots), BF)],
        in_specs=[VMEM, pl.BlockSpec((chunk, model), lambda i: (i, 0))],
        out_specs=[
            pl.BlockSpec((slots, chunk), lambda i: (0, i)),
            pl.BlockSpec((model, slots), lambda i: (0, 0)),
        ],
        scratch_shapes=[pltpu.VMEM((slots, model), BF)],
        compiler_params=BIG,
        name="dact",
    )(grad_wire, down)
    act, partial_grads, dnormed = pl.pallas_call(
        functools.partial(expert_kernel, pairs, parts),
        grid=(blocks,),
        out_shape=[sds((slots, hidden), BF), sds((model, 2 * hidden), BF), wire],
        in_specs=[
            VMEM,
            pl.BlockSpec((model, chunk), lambda i: (0, i)),
            pl.BlockSpec((slots, chunk), lambda i: (0, i)),
            pl.BlockSpec((model, slots), lambda i: (0, 0)),
        ],
        out_specs=[
            pl.BlockSpec((slots, chunk), lambda i: (0, i)),
            pl.BlockSpec((model, 2 * chunk), lambda i: (0, i)),
            whole_wire,
        ],
        scratch_shapes=[
            pltpu.VMEM((slots, model), BF),
            pltpu.VMEM((model, slots), BF),
            pltpu.VMEM((slots, model), F32),
        ],
        compiler_params=BIG,
        name="expert",
    )(wire_rows, up, dact, turned)
    sums = lax.psum_scatter(partial_grads, ("seq", "dp"), scatter_dimension=0, tiled=True)
    dnormed_back = swap(dnormed)
    act_late, _ = lax.optimization_barrier((act, partial_grads))
    produced = pl.pallas_call(
        out_kernel,
        grid=(blocks,),
        out_shape=wire,
        in_specs=[
            pl.BlockSpec((slots, chunk), lambda i: (0, i)),
            pl.BlockSpec((chunk, model), lambda i: (i, 0)),
        ],
        out_specs=whole_wire,
        scratch_shapes=[pltpu.VMEM((slots, model), F32)],
        compiler_params=BIG,
        cost_estimate=HEAVY,
        name="expert_out",
    )(act_late, down)

    dnormed_back, produced = lax.optimization_barrier((dnormed_back, produced))
    grad_pieces = pl.pallas_call(
        functools.partial(dattended_kernel, parts),
        out_shape=[single] * parts,
        in_specs=[SMEM] + [VMEM] * 4,
        out_specs=[VMEM] * parts,
        scratch_shapes=[pltpu.VMEM((tokens, model), BF)],
        name="dattended",
    )(me, place, dnormed_back, attended, cot)
    grad_pieces = exchange(grad_pieces, 1)

    produced_back = swap(produced)

    back_pieces = pl.pallas_call(
        functools.partial(attend_back_kernel, parts),
        out_shape=[triple] * parts,
        in_specs=[VMEM] * (2 * parts + 1),
        out_specs=[VMEM] * parts,
        scratch_shapes=[pltpu.VMEM((length, width), BF)] * 2
        + [pltpu.VMEM((length, width), F32)] * 2,
        compiler_params=BIG,
        cost_estimate=MIDDLE,
        name="attend_back",
    )(*pieces, *grad_pieces, probs)
    back_pieces = exchange(back_pieces, -1)

    band = model // (pairs * parts)
    layer_output, grad_queries, grad_keys, grad_values, grad_up, grad_down = pl.pallas_call(
        functools.partial(finish_kernel, parts, blocks),
        out_shape=[sds((tokens, model), BF)] * 4 + [sds((band, hidden), F32), sds((hidden, band), F32)],
        in_specs=[SMEM] + [VMEM] * (parts + 5),
        out_specs=[VMEM] * 6,
        compiler_params=BIG,
        name="finish",
    )(me, sums, place, produced_back, attended, gate, *back_pieces)
    return (
        layer_output[None],
        grad_queries[None],
        grad_keys[None],
        grad_values[None],
        grad_up[None],
        grad_down[None],
    )


def solution(mesh):
    rows = P(("dp", "expert"), "seq", None)
    weight = P("expert", None, None)
    return jax.shard_map(
        shards,
        mesh=mesh,
        in_specs=(rows, rows, rows, rows, rows, weight, weight, rows),
        out_specs=(rows, rows, rows, rows, P("expert", ("dp", "seq"), None), P("expert", None, ("dp", "seq"))),
        check_vma=False,
    )
```

```python
import functools
import math

import jax
import jax.numpy as jnp
from jax import lax
from jax.experimental import pallas as pl
from jax.experimental.pallas import tpu as pltpu
from jax.sharding import PartitionSpec as P

DH = 128
TOP = 2
EPSILON = 1e-06
GELU_COEF = math.sqrt(2.0 / math.pi)
BF = jnp.bfloat16
F32 = jnp.float32
VMEM = pl.BlockSpec(memory_space=pltpu.VMEM)
SMEM = pl.BlockSpec(memory_space=pltpu.SMEM)
NN = (((1,), (0,)), ((), ()))
NT = (((1,), (1,)), ((), ()))
TN = (((0,), (0,)), ((), ()))
HEAVY = pl.CostEstimate(flops=1_000_000_000_000, transcendentals=0, bytes_accessed=1_000_000)
MIDDLE = pl.CostEstimate(flops=40_000_000_000, transcendentals=0, bytes_accessed=1_000_000)
BIG = pltpu.CompilerParams(vmem_limit_bytes=56 * 1024 * 1024)


def dot(a, b, dims=NN):
    return lax.dot_general(a, b, dims, preferred_element_type=F32)


def sds(shape, dtype):
    return jax.ShapeDtypeStruct(shape, dtype)


def near(array):
    return pltpu.with_memory_space_constraint(array, pltpu.VMEM)


def lane_block(me, step, parts, width):
    return pl.ds(pl.multiple_of(lax.rem(me + step, parts) * width, width), width)


def split_kernel(parts, me_ref, q_ref, k_ref, v_ref, *outs):
    me = me_ref[0]
    rows = q_ref.shape[0]
    width = q_ref.shape[1] // parts
    for step in range(parts):
        lanes = lane_block(me, step, parts, width)
        for i, ref in enumerate((q_ref, k_ref, v_ref)):
            outs[step][i * rows:(i + 1) * rows, :] = ref[:, lanes]


def join_kernel(parts, me_ref, *refs):
    me = me_ref[0]
    pieces, outs = refs[:parts], refs[parts:]
    rows = outs[0].shape[0]
    width = outs[0].shape[1] // parts
    for step in range(parts):
        lanes = lane_block(me, step, parts, width)
        for i, ref in enumerate(outs):
            ref[:, lanes] = pieces[step][i * rows:(i + 1) * rows, :]


def attend_kernel(parts, *refs):
    pieces = refs[:parts]
    outs = refs[parts:2 * parts]
    probs_ref, keys, values = refs[2 * parts:]
    rows = outs[0].shape[0]
    width = outs[0].shape[1]
    scaling = 1.0 / math.sqrt(DH)
    for step in range(parts):
        keys[step * rows:(step + 1) * rows, :] = pieces[step][rows:2 * rows, :]
        values[step * rows:(step + 1) * rows, :] = pieces[step][2 * rows:3 * rows, :]
    for head in range(width // DH):
        lanes = slice(head * DH, (head + 1) * DH)
        for step in range(parts):
            scores = dot(pieces[step][0:rows, lanes], keys[:, lanes], NT) * scaling
            exponent = jnp.exp(scores - jnp.max(scores, axis=-1, keepdims=True))
            probs = exponent / jnp.sum(exponent, axis=-1, keepdims=True)
            rounded = probs.astype(BF)
            probs_ref[head, step * rows:(step + 1) * rows, :] = rounded
            outs[step][:, lanes] = dot(rounded, values[:, lanes]).astype(BF)


def attend_back_kernel(parts, *refs):
    pieces = refs[:parts]
    grads = refs[parts:2 * parts]
    probs_ref = refs[2 * parts]
    outs = refs[2 * parts + 1:3 * parts + 1]
    keys, values, grad_keys, grad_values = refs[3 * parts + 1:]
    rows = grads[0].shape[0]
    width = grads[0].shape[1]
    scaling = 1.0 / math.sqrt(DH)
    for step in range(parts):
        keys[step * rows:(step + 1) * rows, :] = pieces[step][rows:2 * rows, :]
        values[step * rows:(step + 1) * rows, :] = pieces[step][2 * rows:3 * rows, :]
    for head in range(width // DH):
        lanes = slice(head * DH, (head + 1) * DH)
        for step in range(parts):
            query = pieces[step][0:rows, lanes]
            grad = grads[step][:, lanes]
            rounded = probs_ref[head, step * rows:(step + 1) * rows, :]
            probs = rounded.astype(F32)
            grad_probs = dot(grad, values[:, lanes], NT)
            delta = jnp.sum(probs * grad_probs, axis=-1, keepdims=True)
            grad_scores = (probs * (grad_probs - delta) * scaling).astype(BF)
            outs[step][0:rows, lanes] = dot(grad_scores, keys[:, lanes]).astype(BF)
            key_part = dot(grad_scores, query, TN)
            value_part = dot(rounded, grad, TN)
            if step == 0:
                grad_keys[:, lanes] = key_part
                grad_values[:, lanes] = value_part
            else:
                grad_keys[:, lanes] += key_part
                grad_values[:, lanes] += value_part
    for step in range(parts):
        outs[step][rows:2 * rows, :] = grad_keys[step * rows:(step + 1) * rows, :].astype(BF)
        outs[step][2 * rows:3 * rows, :] = grad_values[step * rows:(step + 1) * rows, :].astype(BF)


def chunk_of(array, c):
    return array[:, c * 128:(c + 1) * 128]


def lane_cat(pieces):
    return jnp.concatenate(pieces, axis=1)


def half_pickers(owners):
    shape = (owners * 4, owners * 8)
    row = lax.broadcasted_iota(jnp.int32, shape, 0)
    col = lax.broadcasted_iota(jnp.int32, shape, 1)
    first = lax.shift_left(lax.shift_right_logical(row, 2), 3) + lax.bitwise_and(row, 3)
    return [(col == first + 4 * half).astype(F32).astype(BF) for half in range(2)]


def read_tiles(ref):
    owners, lines, _ = ref.shape
    tiles = [
        ref[:, 8 * t:8 * t + 8, :].astype(F32).reshape(owners * 8, 128).astype(BF)
        for t in range(lines // 8)
    ]
    count = len(tiles) * 2 // 3
    return tiles[:count], lane_cat(tiles[count:])


def write_tiles(ref, low, high):
    owners = ref.shape[0]
    count = low.shape[1] // 128
    for c in range(count):
        ref[:, 8 * c:8 * c + 8, :] = chunk_of(low, c).reshape(owners, 8, 128).astype(BF)
    for c in range(count // 2):
        start = 8 * (count + c)
        ref[:, start:start + 8, :] = chunk_of(high, c).reshape(owners, 8, 128).astype(BF)


def split_parity(array):
    count = array.shape[1] // 128
    return [lane_cat([chunk_of(array, c) for c in range(half, count, 2)]) for half in range(2)]


def merge_parity(even, odd):
    count = even.shape[1] // 128
    return lane_cat([chunk_of(part, c) for c in range(count) for part in (even, odd)])


def unpack_rows(ref, out_ref):
    low, high = read_tiles(ref)
    owners = ref.shape[0]
    even, odd = [dot(pick, high).astype(BF) for pick in half_pickers(owners)]
    out_ref[0:owners * 8, :] = lane_cat(low)
    out_ref[owners * 8:, :] = merge_parity(even, odd)


def pack_rows(rows, ref):
    owners = ref.shape[0]
    pickers = half_pickers(owners)
    parts = split_parity(rows[owners * 8:, :].astype(BF))
    high = dot(pickers[0], parts[0], TN) + dot(pickers[1], parts[1], TN)
    write_tiles(ref, rows[0:owners * 8, :], high)


def pack_tokens(places, arrays, ref):
    low = sum([dot(place[0], x) for place, x in zip(places, arrays)])
    high = None
    for place, x in zip(places, arrays):
        for half, part in enumerate(split_parity(x)):
            term = dot(place[1 + half], part)
            high = term if high is None else high + term
    write_tiles(ref, low, high)


def unpack_tokens(place, low, high):
    even, odd = [dot(place[1 + half], high, TN) for half in range(2)]
    return dot(place[0], lane_cat(low), TN) + merge_parity(even, odd)


def column(row):
    side = row.shape[1]
    return jnp.broadcast_to(row, (side, side)).T[:, 0:1]


def place_kernel(experts, routes_ref, gates_ref, cot_ref, place_ref, packed_ref):
    tokens = cot_ref.shape[0]
    first = lax.broadcasted_iota(jnp.int32, (tokens, tokens), 0)
    second = lax.broadcasted_iota(jnp.int32, (tokens, tokens), 1)
    earlier = (first < second).astype(F32).astype(BF)
    expert_ids = lax.broadcasted_iota(jnp.int32, (experts, tokens), 0)
    line_ids = lax.broadcasted_iota(jnp.int32, (experts * 8, tokens), 0)
    routes = [routes_ref[j:j + 1, :] for j in range(TOP)]
    hits = [(route == expert_ids).astype(F32) for route in routes]
    before = dot(sum(hits[1:], hits[0]).astype(BF), earlier)
    upstream = cot_ref[...].astype(F32)
    places, arrays = [], []
    for j in range(TOP):
        rank = jnp.sum(before * hits[j], axis=0, keepdims=True).astype(jnp.int32)
        line = routes[j] * 8 + rank
        targets = (
            jnp.where(rank < 8, line, -1),
            jnp.where(rank >= 8, line - 8, -1),
            jnp.where(rank >= 8, line - 4, -1),
        )
        place = [(line_ids == target).astype(F32).astype(BF) for target in targets]
        for i, part in enumerate(place):
            place_ref[j, i] = part
        places.append(place)
        arrays.append((column(gates_ref[j:j + 1, :]) * upstream).astype(BF))
    pack_tokens(places, arrays, packed_ref)


def entry_kernel(parts, experts, me_ref, q_ref, k_ref, v_ref, routes_ref, gates_ref, cot_ref, *outs):
    split_kernel(parts, me_ref, q_ref, k_ref, v_ref, *outs[:parts])
    place_kernel(experts, routes_ref, gates_ref, cot_ref, *outs[parts:])


def inverse_rms_of(attended):
    return lax.rsqrt(jnp.mean(attended * attended, axis=-1, keepdims=True) + EPSILON)


def joint_place(place_ref):
    joint = []
    for i in range(3):
        part = place_ref[0, i]
        for j in range(1, TOP):
            part = part + place_ref[j, i]
        joint.append(part)
    return joint


def norm_kernel(parts, me_ref, place_ref, *refs):
    pieces, (attended_ref, packed_ref) = refs[:parts], refs[parts:]
    me = me_ref[0]
    width = pieces[0].shape[1]
    for step in range(parts):
        attended_ref[:, lane_block(me, step, parts, width)] = pieces[step][...]
    attended = attended_ref[...].astype(F32)
    normed = (attended * inverse_rms_of(attended)).astype(BF)
    pack_tokens([joint_place(place_ref)], [normed], packed_ref)


def turn_rows(pairs, parts, rows_ref, turned_ref):
    band = rows_ref.shape[1] // (pairs * parts)
    for s in range(pairs * parts):
        block = (s % pairs) * parts + s // pairs
        turned_ref[s * band:(s + 1) * band, :] = rows_ref[:, block * band:(block + 1) * band].T


def dact_kernel(pairs, parts, packed_ref, down_ref, out_ref, turned_ref, rows):
    @pl.when(pl.program_id(0) == 0)
    def _():
        unpack_rows(packed_ref, rows)
        turn_rows(pairs, parts, rows, turned_ref)

    out_ref[...] = dot(rows[...], down_ref[...], NT)


def expert_kernel(pairs, parts, packed_ref, up_ref, dact_ref, grads_turned_ref, act_ref, grads_ref, dnormed_ref, rows, turned, total):
    step = pl.program_id(0)

    @pl.when(step == 0)
    def _():
        unpack_rows(packed_ref, rows)
        turn_rows(pairs, parts, rows, turned)

    chunk = up_ref.shape[1]
    pre = dot(rows[...], up_ref[...])
    square = pre * pre
    half = 0.5 + 0.5 * jnp.tanh(pre * (GELU_COEF + (GELU_COEF * 0.044715) * square))
    act = pre * half
    act_rounded = act.astype(BF)
    act_ref[...] = act_rounded
    slope = half + act * (1.0 - half) * (2.0 * GELU_COEF + (6.0 * GELU_COEF * 0.044715) * square)
    dpre = (dact_ref[...] * slope).astype(BF)
    grads_ref[:, 0:chunk] = dot(grads_turned_ref[...], act_rounded).astype(BF)
    grads_ref[:, chunk:] = dot(turned[...], dpre).astype(BF)
    part = dot(dpre, up_ref[...], NT)

    @pl.when(step == 0)
    def _():
        total[...] = part

    @pl.when(step > 0)
    def _():
        total[...] += part

    @pl.when(step == pl.num_programs(0) - 1)
    def _():
        pack_rows(total[...], dnormed_ref)


def out_kernel(hidden_ref, weight_ref, packed_ref, total):
    step = pl.program_id(0)
    part = dot(hidden_ref[...], weight_ref[...])

    @pl.when(step == 0)
    def _():
        total[...] = part

    @pl.when(step > 0)
    def _():
        total[...] += part

    @pl.when(step == pl.num_programs(0) - 1)
    def _():
        pack_rows(total[...], packed_ref)


def dattended_kernel(parts, me_ref, place_ref, back_ref, attended_ref, cot_ref, *refs):
    outs, full = refs[:parts], refs[parts]
    me = me_ref[0]
    low, high = read_tiles(back_ref)
    grad_unit = unpack_tokens(joint_place(place_ref), low, high)
    attended = attended_ref[...].astype(F32)
    inverse_rms = inverse_rms_of(attended)
    unit = attended * inverse_rms
    grad = cot_ref[...].astype(F32) + inverse_rms * (
        grad_unit - unit * jnp.mean(grad_unit * unit, axis=-1, keepdims=True)
    )
    full[...] = grad.astype(BF)
    width = outs[0].shape[1]
    for step in range(parts):
        outs[step][...] = full[:, lane_block(me, step, parts, width)]


def mix_kernel(place_ref, back_ref, attended_ref, gates_ref, out_ref):
    low, high = read_tiles(back_ref)
    mix = None
    for j in range(TOP):
        place = [place_ref[j, i] for i in range(3)]
        term = column(gates_ref[j:j + 1, :]) * unpack_tokens(place, low, high)
        mix = term if mix is None else mix + term
    out_ref[...] = (attended_ref[...].astype(F32) + mix).astype(BF)


def widen_kernel(blocks, sums_ref, up_out, down_out):
    chunk = up_out.shape[1] // blocks
    for i in range(blocks):
        start = 2 * i * chunk
        rows = slice(i * chunk, (i + 1) * chunk)
        down_out[rows, :] = sums_ref[:, start:start + chunk].astype(F32).T
        up_out[:, rows] = sums_ref[:, start + chunk:start + 2 * chunk].astype(F32)


def finish_kernel(parts, blocks, me_ref, sums_ref, place_ref, back_ref, attended_ref, gates_ref, *refs):
    pieces, outs = refs[:parts], refs[parts:]
    widen_kernel(blocks, sums_ref, *outs[4:])
    mix_kernel(place_ref, back_ref, attended_ref, gates_ref, outs[0])
    join_kernel(parts, me_ref, *pieces, *outs[1:4])


def shards(query, key, value, routes, gates, up, down, cotangent):
    tokens, model = query.shape[1:]
    owners = lax.axis_size("expert")
    parts = lax.axis_size("seq")
    pairs = lax.axis_size("dp")
    capacity = tokens * TOP * 3 // (2 * owners)
    slots = owners * capacity
    hidden = up.shape[2]
    width = model // parts
    length = tokens * parts
    heads = width // DH
    up, down = up[0], down[0]
    cot = cotangent[0]
    route, gate = routes[0].T, gates[0].T
    me = jnp.reshape(lax.axis_index("seq"), (1,)).astype(jnp.int32)

    def shift(piece, step):
        pairs_of = [(i, (i + step) % parts) for i in range(parts)]
        return near(lax.ppermute(piece, "seq", pairs_of))

    def swap(packed):
        return near(lax.all_to_all(packed, "expert", split_axis=0, concat_axis=0, tiled=True))

    order = (2, 1, 3) if parts == 4 else tuple(range(1, parts))

    def exchange(pieces, sign):
        moved = {step: shift(pieces[step], sign * step) for step in order}
        return [pieces[0]] + [moved[step] for step in range(1, parts)]

    triple = sds((3 * tokens, width), BF)
    single = sds((tokens, width), BF)
    wire = sds((owners, capacity * model // 128, 128), BF)
    *sent, place, packed_grads = pl.pallas_call(
        functools.partial(entry_kernel, parts, owners),
        out_shape=[triple] * parts + [sds((TOP, 3, owners * 8, tokens), BF), wire],
        in_specs=[SMEM] + [VMEM] * 6,
        out_specs=[VMEM] * (parts + 2),
        name="entry",
    )(me, query[0], key[0], value[0], route, gate, cot)
    pieces = exchange(sent, 1)
    grad_wire = swap(packed_grads)

    attended_pieces = pl.pallas_call(
        functools.partial(attend_kernel, parts),
        out_shape=[single] * parts + [sds((heads, length, length), BF)],
        in_specs=[VMEM] * parts,
        out_specs=[VMEM] * (parts + 1),
        scratch_shapes=[pltpu.VMEM((length, width), BF)] * 2,
        compiler_params=BIG,
        cost_estimate=HEAVY,
        name="attend",
    )(*pieces)
    probs = attended_pieces[parts]
    attended_pieces = exchange(attended_pieces[:parts], -1)

    attended, packed = pl.pallas_call(
        functools.partial(norm_kernel, parts),
        out_shape=[sds((tokens, model), BF), wire],
        in_specs=[SMEM] + [VMEM] * (parts + 1),
        out_specs=[VMEM] * 2,
        name="norm_pack",
    )(me, place, *attended_pieces)
    wire_rows = swap(packed)

    blocks = 4
    chunk = hidden // blocks
    whole_wire = pl.BlockSpec(wire.shape, lambda i: (0, 0, 0))
    dact, turned = pl.pallas_call(
        functools.partial(dact_kernel, pairs, parts),
        grid=(blocks,),
        out_shape=[sds((slots, hidden), F32), sds((model, slots), BF)],
        in_specs=[VMEM, pl.BlockSpec((chunk, model), lambda i: (i, 0))],
        out_specs=[
            pl.BlockSpec((slots, chunk), lambda i: (0, i)),
            pl.BlockSpec((model, slots), lambda i: (0, 0)),
        ],
        scratch_shapes=[pltpu.VMEM((slots, model), BF)],
        compiler_params=BIG,
        name="dact",
    )(grad_wire, down)
    act, partial_grads, dnormed = pl.pallas_call(
        functools.partial(expert_kernel, pairs, parts),
        grid=(blocks,),
        out_shape=[sds((slots, hidden), BF), sds((model, 2 * hidden), BF), wire],
        in_specs=[
            VMEM,
            pl.BlockSpec((model, chunk), lambda i: (0, i)),
            pl.BlockSpec((slots, chunk), lambda i: (0, i)),
            pl.BlockSpec((model, slots), lambda i: (0, 0)),
        ],
        out_specs=[
            pl.BlockSpec((slots, chunk), lambda i: (0, i)),
            pl.BlockSpec((model, 2 * chunk), lambda i: (0, i)),
            whole_wire,
        ],
        scratch_shapes=[
            pltpu.VMEM((slots, model), BF),
            pltpu.VMEM((model, slots), BF),
            pltpu.VMEM((slots, model), F32),
        ],
        compiler_params=BIG,
        name="expert",
    )(wire_rows, up, dact, turned)
    sums = lax.psum_scatter(partial_grads, ("seq", "dp"), scatter_dimension=0, tiled=True)
    dnormed_back = swap(dnormed)
    act_late, _ = lax.optimization_barrier((act, partial_grads))
    produced = pl.pallas_call(
        out_kernel,
        grid=(blocks,),
        out_shape=wire,
        in_specs=[
            pl.BlockSpec((slots, chunk), lambda i: (0, i)),
            pl.BlockSpec((chunk, model), lambda i: (i, 0)),
        ],
        out_specs=whole_wire,
        scratch_shapes=[pltpu.VMEM((slots, model), F32)],
        compiler_params=BIG,
        cost_estimate=HEAVY,
        name="expert_out",
    )(act_late, down)

    dnormed_back, produced = lax.optimization_barrier((dnormed_back, produced))
    grad_pieces = pl.pallas_call(
        functools.partial(dattended_kernel, parts),
        out_shape=[single] * parts,
        in_specs=[SMEM] + [VMEM] * 4,
        out_specs=[VMEM] * parts,
        scratch_shapes=[pltpu.VMEM((tokens, model), BF)],
        name="dattended",
    )(me, near(place), dnormed_back, near(attended), near(cot))
    grad_pieces = exchange(grad_pieces, 1)

    produced_back = swap(produced)

    back_pieces = pl.pallas_call(
        functools.partial(attend_back_kernel, parts),
        out_shape=[triple] * parts,
        in_specs=[VMEM] * (2 * parts + 1),
        out_specs=[VMEM] * parts,
        scratch_shapes=[pltpu.VMEM((length, width), BF)] * 2
        + [pltpu.VMEM((length, width), F32)] * 2,
        compiler_params=BIG,
        cost_estimate=MIDDLE,
        name="attend_back",
    )(*pieces, *grad_pieces, probs)
    back_pieces = exchange(back_pieces, -1)

    band = model // (pairs * parts)
    layer_output, grad_queries, grad_keys, grad_values, grad_up, grad_down = pl.pallas_call(
        functools.partial(finish_kernel, parts, blocks),
        out_shape=[sds((tokens, model), BF)] * 4 + [sds((band, hidden), F32), sds((hidden, band), F32)],
        in_specs=[SMEM] + [VMEM] * (parts + 5),
        out_specs=[VMEM] * 6,
        compiler_params=BIG,
        name="finish",
    )(me, sums, near(place), produced_back, near(attended), gate, *back_pieces)
    return (
        layer_output[None],
        grad_queries[None],
        grad_keys[None],
        grad_values[None],
        grad_up[None],
        grad_down[None],
    )


def solution(mesh):
    rows = P(("dp", "expert"), "seq", None)
    weight = P("expert", None, None)
    return jax.shard_map(
        shards,
        mesh=mesh,
        in_specs=(rows, rows, rows, rows, rows, weight, weight, rows),
        out_specs=(rows, rows, rows, rows, P("expert", ("dp", "seq"), None), P("expert", None, ("dp", "seq"))),
        check_vma=False,
    )
```

```python
import functools
import math

import jax
import jax.numpy as jnp
from jax import lax
from jax.experimental import pallas as pl
from jax.experimental.pallas import tpu as pltpu
from jax.sharding import PartitionSpec as P

DH = 128
TOP = 2
EPSILON = 1e-06
GELU_COEF = math.sqrt(2.0 / math.pi)
BF = jnp.bfloat16
F32 = jnp.float32
VMEM = pl.BlockSpec(memory_space=pltpu.VMEM)
SMEM = pl.BlockSpec(memory_space=pltpu.SMEM)
NN = (((1,), (0,)), ((), ()))
NT = (((1,), (1,)), ((), ()))
TN = (((0,), (0,)), ((), ()))
HEAVY = pl.CostEstimate(flops=1_000_000_000_000, transcendentals=0, bytes_accessed=1_000_000)
MIDDLE = pl.CostEstimate(flops=40_000_000_000, transcendentals=0, bytes_accessed=1_000_000)
BIG = pltpu.CompilerParams(vmem_limit_bytes=56 * 1024 * 1024)


def dot(a, b, dims=NN):
    return lax.dot_general(a, b, dims, preferred_element_type=F32)


def sds(shape, dtype):
    return jax.ShapeDtypeStruct(shape, dtype)


def near(array):
    return pltpu.with_memory_space_constraint(array, pltpu.VMEM)


def lane_block(me, step, parts, width):
    return pl.ds(pl.multiple_of(lax.rem(me + step, parts) * width, width), width)


def split_kernel(parts, me_ref, q_ref, k_ref, v_ref, *outs):
    me = me_ref[0]
    rows = q_ref.shape[0]
    width = q_ref.shape[1] // parts
    for step in range(parts):
        lanes = lane_block(me, step, parts, width)
        for i, ref in enumerate((q_ref, k_ref, v_ref)):
            outs[step][i * rows:(i + 1) * rows, :] = ref[:, lanes]


def join_kernel(parts, me_ref, *refs):
    me = me_ref[0]
    pieces, outs = refs[:parts], refs[parts:]
    rows = outs[0].shape[0]
    width = outs[0].shape[1] // parts
    for step in range(parts):
        lanes = lane_block(me, step, parts, width)
        for i, ref in enumerate(outs):
            ref[:, lanes] = pieces[step][i * rows:(i + 1) * rows, :]


def attend_kernel(parts, *refs):
    pieces = refs[:parts]
    outs = refs[parts:2 * parts]
    probs_ref, keys, values = refs[2 * parts:]
    rows = outs[0].shape[0]
    width = outs[0].shape[1]
    scaling = 1.0 / math.sqrt(DH)
    for step in range(parts):
        keys[step * rows:(step + 1) * rows, :] = pieces[step][rows:2 * rows, :]
        values[step * rows:(step + 1) * rows, :] = pieces[step][2 * rows:3 * rows, :]
    for head in range(width // DH):
        lanes = slice(head * DH, (head + 1) * DH)
        for step in range(parts):
            scores = dot(pieces[step][0:rows, lanes], keys[:, lanes], NT) * scaling
            exponent = jnp.exp(scores - jnp.max(scores, axis=-1, keepdims=True))
            probs = exponent / jnp.sum(exponent, axis=-1, keepdims=True)
            rounded = probs.astype(BF)
            probs_ref[head, step * rows:(step + 1) * rows, :] = rounded
            outs[step][:, lanes] = dot(rounded, values[:, lanes]).astype(BF)


def attend_back_kernel(parts, *refs):
    pieces = refs[:parts]
    grads = refs[parts:2 * parts]
    probs_ref = refs[2 * parts]
    outs = refs[2 * parts + 1:3 * parts + 1]
    keys, values, grad_keys, grad_values = refs[3 * parts + 1:]
    rows = grads[0].shape[0]
    width = grads[0].shape[1]
    scaling = 1.0 / math.sqrt(DH)
    for step in range(parts):
        keys[step * rows:(step + 1) * rows, :] = pieces[step][rows:2 * rows, :]
        values[step * rows:(step + 1) * rows, :] = pieces[step][2 * rows:3 * rows, :]
    for head in range(width // DH):
        lanes = slice(head * DH, (head + 1) * DH)
        for step in range(parts):
            query = pieces[step][0:rows, lanes]
            grad = grads[step][:, lanes]
            rounded = probs_ref[head, step * rows:(step + 1) * rows, :]
            probs = rounded.astype(F32)
            grad_probs = dot(grad, values[:, lanes], NT)
            delta = jnp.sum(probs * grad_probs, axis=-1, keepdims=True)
            grad_scores = (probs * (grad_probs - delta) * scaling).astype(BF)
            outs[step][0:rows, lanes] = dot(grad_scores, keys[:, lanes]).astype(BF)
            key_part = dot(grad_scores, query, TN)
            value_part = dot(rounded, grad, TN)
            if step == 0:
                grad_keys[:, lanes] = key_part
                grad_values[:, lanes] = value_part
            else:
                grad_keys[:, lanes] += key_part
                grad_values[:, lanes] += value_part
    for step in range(parts):
        outs[step][rows:2 * rows, :] = grad_keys[step * rows:(step + 1) * rows, :].astype(BF)
        outs[step][2 * rows:3 * rows, :] = grad_values[step * rows:(step + 1) * rows, :].astype(BF)


def chunk_of(array, c):
    return array[:, c * 128:(c + 1) * 128]


def lane_cat(pieces):
    return jnp.concatenate(pieces, axis=1)


def half_pickers(owners):
    shape = (owners * 4, owners * 8)
    row = lax.broadcasted_iota(jnp.int32, shape, 0)
    col = lax.broadcasted_iota(jnp.int32, shape, 1)
    first = lax.shift_left(lax.shift_right_logical(row, 2), 3) + lax.bitwise_and(row, 3)
    return [(col == first + 4 * half).astype(F32).astype(BF) for half in range(2)]


def read_tiles(ref):
    owners, lines, _ = ref.shape
    tiles = [
        ref[:, 8 * t:8 * t + 8, :].astype(F32).reshape(owners * 8, 128).astype(BF)
        for t in range(lines // 8)
    ]
    count = len(tiles) * 2 // 3
    return tiles[:count], lane_cat(tiles[count:])


def write_tiles(ref, low, high):
    owners = ref.shape[0]
    count = low.shape[1] // 128
    for c in range(count):
        ref[:, 8 * c:8 * c + 8, :] = chunk_of(low, c).reshape(owners, 8, 128).astype(BF)
    for c in range(count // 2):
        start = 8 * (count + c)
        ref[:, start:start + 8, :] = chunk_of(high, c).reshape(owners, 8, 128).astype(BF)


def split_parity(array):
    count = array.shape[1] // 128
    return [lane_cat([chunk_of(array, c) for c in range(half, count, 2)]) for half in range(2)]


def merge_parity(even, odd):
    count = even.shape[1] // 128
    return lane_cat([chunk_of(part, c) for c in range(count) for part in (even, odd)])


def unpack_rows(ref, out_ref):
    low, high = read_tiles(ref)
    owners = ref.shape[0]
    even, odd = [dot(pick, high).astype(BF) for pick in half_pickers(owners)]
    out_ref[0:owners * 8, :] = lane_cat(low)
    out_ref[owners * 8:, :] = merge_parity(even, odd)


def pack_rows(rows, ref):
    owners = ref.shape[0]
    pickers = half_pickers(owners)
    parts = split_parity(rows[owners * 8:, :].astype(BF))
    high = dot(pickers[0], parts[0], TN) + dot(pickers[1], parts[1], TN)
    write_tiles(ref, rows[0:owners * 8, :], high)


def pack_tokens(places, arrays, ref):
    low = sum([dot(place[0], x) for place, x in zip(places, arrays)])
    high = None
    for place, x in zip(places, arrays):
        for half, part in enumerate(split_parity(x)):
            term = dot(place[1 + half], part)
            high = term if high is None else high + term
    write_tiles(ref, low, high)


def unpack_tokens(place, low, high):
    even, odd = [dot(place[1 + half], high, TN) for half in range(2)]
    return dot(place[0], lane_cat(low), TN) + merge_parity(even, odd)


def column(row):
    side = row.shape[1]
    return jnp.broadcast_to(row, (side, side)).T[:, 0:1]


def place_kernel(experts, routes_ref, gates_ref, cot_ref, place_ref, packed_ref):
    tokens = cot_ref.shape[0]
    first = lax.broadcasted_iota(jnp.int32, (tokens, tokens), 0)
    second = lax.broadcasted_iota(jnp.int32, (tokens, tokens), 1)
    earlier = (first < second).astype(F32).astype(BF)
    expert_ids = lax.broadcasted_iota(jnp.int32, (experts, tokens), 0)
    line_ids = lax.broadcasted_iota(jnp.int32, (experts * 8, tokens), 0)
    routes = [routes_ref[j:j + 1, :] for j in range(TOP)]
    hits = [(route == expert_ids).astype(F32) for route in routes]
    before = dot(sum(hits[1:], hits[0]).astype(BF), earlier)
    upstream = cot_ref[...].astype(F32)
    places, arrays = [], []
    for j in range(TOP):
        rank = jnp.sum(before * hits[j], axis=0, keepdims=True).astype(jnp.int32)
        line = routes[j] * 8 + rank
        targets = (
            jnp.where(rank < 8, line, -1),
            jnp.where(rank >= 8, line - 8, -1),
            jnp.where(rank >= 8, line - 4, -1),
        )
        place = [(line_ids == target).astype(F32).astype(BF) for target in targets]
        for i, part in enumerate(place):
            place_ref[j, i] = part
        places.append(place)
        arrays.append((column(gates_ref[j:j + 1, :]) * upstream).astype(BF))
    pack_tokens(places, arrays, packed_ref)


def entry_kernel(parts, experts, me_ref, q_ref, k_ref, v_ref, routes_ref, gates_ref, cot_ref, *outs):
    split_kernel(parts, me_ref, q_ref, k_ref, v_ref, *outs[:parts])
    place_kernel(experts, routes_ref, gates_ref, cot_ref, *outs[parts:])


def inverse_rms_of(attended):
    return lax.rsqrt(jnp.mean(attended * attended, axis=-1, keepdims=True) + EPSILON)


def joint_place(place_ref):
    joint = []
    for i in range(3):
        part = place_ref[0, i]
        for j in range(1, TOP):
            part = part + place_ref[j, i]
        joint.append(part)
    return joint


def norm_kernel(parts, me_ref, place_ref, *refs):
    pieces, (attended_ref, packed_ref) = refs[:parts], refs[parts:]
    me = me_ref[0]
    width = pieces[0].shape[1]
    for step in range(parts):
        attended_ref[:, lane_block(me, step, parts, width)] = pieces[step][...]
    attended = attended_ref[...].astype(F32)
    normed = (attended * inverse_rms_of(attended)).astype(BF)
    pack_tokens([joint_place(place_ref)], [normed], packed_ref)


def turn_rows(pairs, parts, rows_ref, turned_ref):
    band = rows_ref.shape[1] // (pairs * parts)
    for s in range(pairs * parts):
        block = (s % pairs) * parts + s // pairs
        turned_ref[s * band:(s + 1) * band, :] = rows_ref[:, block * band:(block + 1) * band].T


def dact_kernel(pairs, parts, packed_ref, down_ref, out_ref, turned_ref, rows):
    @pl.when(pl.program_id(0) == 0)
    def _():
        unpack_rows(packed_ref, rows)
        turn_rows(pairs, parts, rows, turned_ref)

    out_ref[...] = dot(rows[...], down_ref[...], NT).astype(BF)


def expert_kernel(pairs, parts, packed_ref, up_ref, dact_ref, grads_turned_ref, act_ref, grads_ref, dnormed_ref, rows, turned, total):
    step = pl.program_id(0)

    @pl.when(step == 0)
    def _():
        unpack_rows(packed_ref, rows)
        turn_rows(pairs, parts, rows, turned)

    chunk = up_ref.shape[1]
    pre = dot(rows[...], up_ref[...])
    square = pre * pre
    half = 0.5 + 0.5 * jnp.tanh(pre * (GELU_COEF + (GELU_COEF * 0.044715) * square))
    act = pre * half
    act_rounded = act.astype(BF)
    act_ref[...] = act_rounded
    slope = half + act * (1.0 - half) * (2.0 * GELU_COEF + (6.0 * GELU_COEF * 0.044715) * square)
    dpre = (dact_ref[...].astype(F32) * slope).astype(BF)
    grads_ref[:, 0:chunk] = dot(grads_turned_ref[...], act_rounded).astype(BF)
    grads_ref[:, chunk:] = dot(turned[...], dpre).astype(BF)
    part = dot(dpre, up_ref[...], NT)

    @pl.when(step == 0)
    def _():
        total[...] = part

    @pl.when(step > 0)
    def _():
        total[...] += part

    @pl.when(step == pl.num_programs(0) - 1)
    def _():
        pack_rows(total[...], dnormed_ref)


def out_kernel(hidden_ref, weight_ref, packed_ref, total):
    step = pl.program_id(0)
    part = dot(hidden_ref[...], weight_ref[...])

    @pl.when(step == 0)
    def _():
        total[...] = part

    @pl.when(step > 0)
    def _():
        total[...] += part

    @pl.when(step == pl.num_programs(0) - 1)
    def _():
        pack_rows(total[...], packed_ref)


def dattended_kernel(parts, me_ref, place_ref, back_ref, attended_ref, cot_ref, *refs):
    outs, full = refs[:parts], refs[parts]
    me = me_ref[0]
    low, high = read_tiles(back_ref)
    grad_unit = unpack_tokens(joint_place(place_ref), low, high)
    attended = attended_ref[...].astype(F32)
    inverse_rms = inverse_rms_of(attended)
    unit = attended * inverse_rms
    grad = cot_ref[...].astype(F32) + inverse_rms * (
        grad_unit - unit * jnp.mean(grad_unit * unit, axis=-1, keepdims=True)
    )
    full[...] = grad.astype(BF)
    width = outs[0].shape[1]
    for step in range(parts):
        outs[step][...] = full[:, lane_block(me, step, parts, width)]


def mix_kernel(place_ref, back_ref, attended_ref, gates_ref, out_ref):
    low, high = read_tiles(back_ref)
    mix = None
    for j in range(TOP):
        place = [place_ref[j, i] for i in range(3)]
        term = column(gates_ref[j:j + 1, :]) * unpack_tokens(place, low, high)
        mix = term if mix is None else mix + term
    out_ref[...] = (attended_ref[...].astype(F32) + mix).astype(BF)


def widen_kernel(blocks, sums_ref, up_out, down_out):
    chunk = up_out.shape[1] // blocks
    for i in range(blocks):
        start = 2 * i * chunk
        rows = slice(i * chunk, (i + 1) * chunk)
        down_out[rows, :] = sums_ref[:, start:start + chunk].astype(F32).T
        up_out[:, rows] = sums_ref[:, start + chunk:start + 2 * chunk].astype(F32)


def finish_kernel(parts, blocks, me_ref, sums_ref, place_ref, back_ref, attended_ref, gates_ref, *refs):
    pieces, outs = refs[:parts], refs[parts:]
    widen_kernel(blocks, sums_ref, *outs[4:])
    mix_kernel(place_ref, back_ref, attended_ref, gates_ref, outs[0])
    join_kernel(parts, me_ref, *pieces, *outs[1:4])


def shards(query, key, value, routes, gates, up, down, cotangent):
    tokens, model = query.shape[1:]
    owners = lax.axis_size("expert")
    parts = lax.axis_size("seq")
    pairs = lax.axis_size("dp")
    capacity = tokens * TOP * 3 // (2 * owners)
    slots = owners * capacity
    hidden = up.shape[2]
    width = model // parts
    length = tokens * parts
    heads = width // DH
    up, down = up[0], down[0]
    cot = cotangent[0]
    route, gate = routes[0].T, gates[0].T
    me = jnp.reshape(lax.axis_index("seq"), (1,)).astype(jnp.int32)

    def shift(piece, step):
        pairs_of = [(i, (i + step) % parts) for i in range(parts)]
        return near(lax.ppermute(piece, "seq", pairs_of))

    def swap(packed):
        return near(lax.all_to_all(packed, "expert", split_axis=0, concat_axis=0, tiled=True))

    order = (2, 1, 3) if parts == 4 else tuple(range(1, parts))

    def exchange(pieces, sign):
        moved = {step: shift(pieces[step], sign * step) for step in order}
        return [pieces[0]] + [moved[step] for step in range(1, parts)]

    triple = sds((3 * tokens, width), BF)
    single = sds((tokens, width), BF)
    wire = sds((owners, capacity * model // 128, 128), BF)
    *sent, place, packed_grads = pl.pallas_call(
        functools.partial(entry_kernel, parts, owners),
        out_shape=[triple] * parts + [sds((TOP, 3, owners * 8, tokens), BF), wire],
        in_specs=[SMEM] + [VMEM] * 6,
        out_specs=[VMEM] * (parts + 2),
        name="entry",
    )(me, query[0], key[0], value[0], route, gate, cot)
    pieces = exchange(sent, 1)
    grad_wire = swap(packed_grads)

    attended_pieces = pl.pallas_call(
        functools.partial(attend_kernel, parts),
        out_shape=[single] * parts + [sds((heads, length, length), BF)],
        in_specs=[VMEM] * parts,
        out_specs=[VMEM] * (parts + 1),
        scratch_shapes=[pltpu.VMEM((length, width), BF)] * 2,
        compiler_params=BIG,
        cost_estimate=HEAVY,
        name="attend",
    )(*pieces)
    probs = attended_pieces[parts]
    attended_pieces = exchange(attended_pieces[:parts], -1)

    attended, packed = pl.pallas_call(
        functools.partial(norm_kernel, parts),
        out_shape=[sds((tokens, model), BF), wire],
        in_specs=[SMEM] + [VMEM] * (parts + 1),
        out_specs=[VMEM] * 2,
        name="norm_pack",
    )(me, place, *attended_pieces)
    wire_rows = swap(packed)

    blocks = 4
    chunk = hidden // blocks
    whole_wire = pl.BlockSpec(wire.shape, lambda i: (0, 0, 0))
    dact, turned = pl.pallas_call(
        functools.partial(dact_kernel, pairs, parts),
        grid=(blocks,),
        out_shape=[sds((slots, hidden), BF), sds((model, slots), BF)],
        in_specs=[VMEM, pl.BlockSpec((chunk, model), lambda i: (i, 0))],
        out_specs=[
            pl.BlockSpec((slots, chunk), lambda i: (0, i)),
            pl.BlockSpec((model, slots), lambda i: (0, 0)),
        ],
        scratch_shapes=[pltpu.VMEM((slots, model), BF)],
        compiler_params=BIG,
        name="dact",
    )(grad_wire, down)
    act, partial_grads, dnormed = pl.pallas_call(
        functools.partial(expert_kernel, pairs, parts),
        grid=(blocks,),
        out_shape=[sds((slots, hidden), BF), sds((model, 2 * hidden), BF), wire],
        in_specs=[
            VMEM,
            pl.BlockSpec((model, chunk), lambda i: (0, i)),
            pl.BlockSpec((slots, chunk), lambda i: (0, i)),
            pl.BlockSpec((model, slots), lambda i: (0, 0)),
        ],
        out_specs=[
            pl.BlockSpec((slots, chunk), lambda i: (0, i)),
            pl.BlockSpec((model, 2 * chunk), lambda i: (0, i)),
            whole_wire,
        ],
        scratch_shapes=[
            pltpu.VMEM((slots, model), BF),
            pltpu.VMEM((model, slots), BF),
            pltpu.VMEM((slots, model), F32),
        ],
        compiler_params=BIG,
        name="expert",
    )(wire_rows, up, dact, turned)
    sums = lax.psum_scatter(partial_grads, ("seq", "dp"), scatter_dimension=0, tiled=True)
    dnormed_back = swap(dnormed)
    act_late, _ = lax.optimization_barrier((act, partial_grads))
    produced = pl.pallas_call(
        out_kernel,
        grid=(blocks,),
        out_shape=wire,
        in_specs=[
            pl.BlockSpec((slots, chunk), lambda i: (0, i)),
            pl.BlockSpec((chunk, model), lambda i: (i, 0)),
        ],
        out_specs=whole_wire,
        scratch_shapes=[pltpu.VMEM((slots, model), F32)],
        compiler_params=BIG,
        cost_estimate=HEAVY,
        name="expert_out",
    )(act_late, down)

    dnormed_back, produced = lax.optimization_barrier((dnormed_back, produced))
    grad_pieces = pl.pallas_call(
        functools.partial(dattended_kernel, parts),
        out_shape=[single] * parts,
        in_specs=[SMEM] + [VMEM] * 4,
        out_specs=[VMEM] * parts,
        scratch_shapes=[pltpu.VMEM((tokens, model), BF)],
        name="dattended",
    )(me, place, dnormed_back, attended, cot)
    grad_pieces = exchange(grad_pieces, 1)

    produced_back = swap(produced)

    back_pieces = pl.pallas_call(
        functools.partial(attend_back_kernel, parts),
        out_shape=[triple] * parts,
        in_specs=[VMEM] * (2 * parts + 1),
        out_specs=[VMEM] * parts,
        scratch_shapes=[pltpu.VMEM((length, width), BF)] * 2
        + [pltpu.VMEM((length, width), F32)] * 2,
        compiler_params=BIG,
        cost_estimate=MIDDLE,
        name="attend_back",
    )(*pieces, *grad_pieces, probs)
    back_pieces = exchange(back_pieces, -1)

    band = model // (pairs * parts)
    layer_output, grad_queries, grad_keys, grad_values, grad_up, grad_down = pl.pallas_call(
        functools.partial(finish_kernel, parts, blocks),
        out_shape=[sds((tokens, model), BF)] * 4 + [sds((band, hidden), F32), sds((hidden, band), F32)],
        in_specs=[SMEM] + [VMEM] * (parts + 5),
        out_specs=[VMEM] * 6,
        compiler_params=BIG,
        name="finish",
    )(me, sums, place, produced_back, attended, gate, *back_pieces)
    return (
        layer_output[None],
        grad_queries[None],
        grad_keys[None],
        grad_values[None],
        grad_up[None],
        grad_down[None],
    )


def solution(mesh):
    rows = P(("dp", "expert"), "seq", None)
    weight = P("expert", None, None)
    return jax.shard_map(
        shards,
        mesh=mesh,
        in_specs=(rows, rows, rows, rows, rows, weight, weight, rows),
        out_specs=(rows, rows, rows, rows, P("expert", ("dp", "seq"), None), P("expert", None, ("dp", "seq"))),
        check_vma=False,
    )
```
